1024 devices in a mesh: ctx: 64 (over z, x), tp: 16 (over y, core).
Axes of the slice: x: 8, y: 8, z: 8, core: 2. Of those that a mesh axis runs over, the one named last changes fastest.
Arguments:
- projected: bfloat16 [3, 16384, 8192], P(None, 'ctx', 'tp'), may hold values from -6 to 6
- short_filter: float32 [3, 7, 512], P(None, None, 'tp'), may hold values from -2 to 2
- long_filter: bfloat16 [128, 512], P(None, 'tp'), may hold values from -0.5 to 0.5
- out_weight: bfloat16 [8192, 8192], P('tp'), may hold values from -0.0625 to 0.0625
- out_grad: bfloat16 [16384, 8192], P(('ctx', 'tp')), may hold values from -6 to 6
Outputs:
- projected_grad: bfloat16 [3, 16384, 8192], P(None, 'ctx', 'tp')
- short_grad: float32 [3, 7, 512], P(None, None, 'tp')
- long_grad: float32 [128, 512], P(None, 'tp')
The draws below stay inside these ranges and needn't reach their ends.
All inputs are finite; a program needn't handle non-finite values.
Results may differ from the reference program's by a relative error of at most 0.013.
Values may be sent and summed in bfloat16 or wider, within the bound.
A program may use at most 64 MiB of HBM per device.

```python
import math
import jax
import jax.numpy as jnp
from jax import lax

D = 8192
GROUP = 16
SHORT = 7
LONG = 128
TOKENS = 16384
G = 512


def steps_of(own_key, shape, shards, low, largest):
    level = 1.0
    for position, parts in shards:
        draws = jax.random.uniform(jax.random.fold_in(jax.random.fold_in(own_key, 6), position), (parts,), jnp.float32, low / len(shards), largest / len(shards))
        level = level * jnp.repeat(jnp.exp(draws), shape[position] // parts).reshape((-1,) + (1,) * (len(shape) - 1 - position))
    return level


def bell_draw(own_key, shape, deviation, bound, shards=(), held_as=jnp.bfloat16):
    array = jax.random.normal(own_key, shape, jnp.float32) * deviation
    if len(shards) > 0:
        array = steps_of(own_key, shape, shards, -0.22, 0.18) * array
    return jnp.clip(array, min=-bound, max=bound).astype(held_as)


def setup_inputs(seed: int = 0) -> dict:
    keys = jax.random.split(jax.random.key(seed), 6)
    return {
        "projected": bell_draw(keys[0], (3, TOKENS, D), 1.0, 6.0, ((1, 64), (2, 16))),
        "short_filter": bell_draw(keys[1], (3, SHORT, G), 0.4, 2.0, ((2, 16),), jnp.float32),
        "long_filter": bell_draw(keys[2], (LONG, G), LONG ** -0.5, 0.5, ((1, 16),)),
        "out_weight": bell_draw(keys[3], (D, D), D ** -0.5, 0.0625, ((0, 16),)),
        "out_grad": bell_draw(keys[4], (TOKENS, D), 1.0, 6.0, ((0, 1024),)),
    }


def filter_matrix(taps, forward):
    length = taps.shape[0]
    lines = jnp.arange(length, dtype=jnp.int32)[:, None]
    places = jnp.arange(2 * length - 1, dtype=jnp.int32)[None, :]
    offset = lines + length - 1 - places if forward else places - lines
    valid = (offset >= 0) & (offset < length)
    index = jnp.clip(offset, 0, length - 1)
    return jnp.where(valid[None], taps.T[:, index], jnp.zeros((), taps.dtype))

def long_apply(extended, matrix):
    length = matrix.shape[1]
    groups = matrix.shape[0]
    channels = extended.shape[1]
    count = extended.shape[0] - (length - 1)
    columns = extended.T

    def one_block(block):
        window = lax.dynamic_slice_in_dim(columns, block * length, 2 * length - 1, 1)
        window = window.reshape(groups, channels // groups, 2 * length - 1)
        result = jnp.einsum('gtj,gcj->gct', matrix, window, preferred_element_type=jnp.float32)
        return result.reshape(channels, length)
    blocks = jnp.arange(count // length, dtype=jnp.int32)
    stacked = lax.map(one_block, blocks)
    return jnp.transpose(stacked, (1, 0, 2)).reshape(channels, count).T

def long_filter_grad(grads, extended, groups):
    count = grads.shape[0]
    channels = grads.shape[1]
    length = extended.shape[0] - count + 1
    grad_cols = grads.T
    ext_cols = extended.T

    def one_block(block):
        window = lax.dynamic_slice_in_dim(ext_cols, block * length, 2 * length - 1, 1)
        window = window.reshape(groups, channels // groups, 2 * length - 1)
        part = lax.dynamic_slice_in_dim(grad_cols, block * length, length, 1)
        part = part.reshape(groups, channels // groups, length)
        table = jnp.einsum('gct,gcj->gtj', part, window, preferred_element_type=jnp.float32)
        flat = table.reshape(groups, length * (2 * length - 1))
        flat = jnp.pad(flat, ((0, 0), (0, length))).reshape(groups, length, 2 * length)
        return lax.optimization_barrier(jnp.sum(flat[:, :, :length], axis=1))
    blocks = jnp.arange(count // length, dtype=jnp.int32)
    sums = lax.optimization_barrier(jnp.sum(lax.map(one_block, blocks), axis=0))
    return sums[:, ::-1].T

def short_apply(extended, taps_ch):
    size = taps_ch.shape[1]
    count = extended.shape[1] - (size - 1)
    total = jnp.zeros((3, count, extended.shape[2]), jnp.float32)
    for tap in range(size):
        start = size - 1 - tap
        total = total + taps_ch[:, tap, None, :] * extended[:, start:start + count].astype(jnp.float32)
    return total

def short_back(extended, taps_ch):
    size = taps_ch.shape[1]
    count = extended.shape[1] - (size - 1)
    total = jnp.zeros((3, count, extended.shape[2]), jnp.float32)
    for tap in range(size):
        total = total + taps_ch[:, tap, None, :] * extended[:, tap:tap + count].astype(jnp.float32)
    return total

def short_filter_grad(grads, extended, groups):
    count = grads.shape[1]
    size = extended.shape[1] - count + 1
    channels = grads.shape[2]
    grads_wide = grads.astype(jnp.float32)
    pieces = []
    for tap in range(size):
        start = size - 1 - tap
        pieces.append(lax.optimization_barrier(jnp.sum(grads_wide * extended[:, start:start + count].astype(jnp.float32), axis=1)))
    stacked = jnp.stack(pieces, axis=1)
    return lax.optimization_barrier(jnp.sum(stacked.reshape(3, size, groups, channels // groups), axis=3))

def reference(projected, short_filter, long_filter, out_weight, out_grad):
    short_ch = jnp.repeat(short_filter, GROUP, axis=2)
    extended = jnp.concatenate([jnp.zeros((3, SHORT - 1, D), jnp.bfloat16), projected], 1)
    mixed = short_apply(extended, short_ch).astype(jnp.bfloat16)
    query, key_part, value = (mixed[0], mixed[1], mixed[2])
    product = (key_part.astype(jnp.float32) * value.astype(jnp.float32)).astype(jnp.bfloat16)
    padded = jnp.concatenate([jnp.zeros((LONG - 1, D), jnp.bfloat16), product], 0)
    forward_mat = filter_matrix(long_filter, True)
    backward_mat = filter_matrix(long_filter, False)
    response = long_apply(padded, forward_mat)
    out_branch = lax.dot_general(out_grad, out_weight, (((1,), (1,)), ((), ())), preferred_element_type=jnp.float32).astype(jnp.bfloat16)
    branch_wide = out_branch.astype(jnp.float32)
    grad_query = (branch_wide * response).astype(jnp.bfloat16)
    grad_resp = (branch_wide * query.astype(jnp.float32)).astype(jnp.bfloat16)
    tail_pad = jnp.concatenate([grad_resp, jnp.zeros((LONG - 1, D), jnp.bfloat16)], 0)
    grad_prod = long_apply(tail_pad, backward_mat).astype(jnp.bfloat16)
    prod_wide = grad_prod.astype(jnp.float32)
    grad_key = (prod_wide * value.astype(jnp.float32)).astype(jnp.bfloat16)
    grad_value = (prod_wide * key_part.astype(jnp.float32)).astype(jnp.bfloat16)
    grad_mixed = jnp.stack([grad_query, grad_key, grad_value], axis=0)
    grad_ext = jnp.concatenate([grad_mixed, jnp.zeros((3, SHORT - 1, D), jnp.bfloat16)], 1)
    projected_grad = short_back(grad_ext, short_ch).astype(jnp.bfloat16)
    scale = 1.0 / math.sqrt(TOKENS * GROUP)
    long_grad = long_filter_grad(grad_resp, padded, D // GROUP) * scale
    short_grad = short_filter_grad(grad_mixed, extended, D // GROUP) * scale
    return (projected_grad, short_grad, long_grad)
```

```python
import functools
import math

import jax
import jax.numpy as jnp
from jax import lax
from jax.experimental import pallas as pl
from jax.experimental.pallas import tpu as pltpu
from jax.sharding import PartitionSpec as P

MESH = pl.DeviceIdType.MESH
BF = jnp.bfloat16
F32 = jnp.float32
HALO = 144
LB = 128
NT = (((1,), (1,)), ((), ()))
TN = (((0,), (0,)), ((), ()))
HI = lax.Precision.HIGHEST


def one_hot(shape, test):
    rows = lax.broadcasted_iota(jnp.int32, shape, 0)
    cols = lax.broadcasted_iota(jnp.int32, shape, 1)
    return jnp.where(test(rows, cols), 1.0, 0.0)


def kernel(
    dims,
    scale,
    proj_hbm,
    sf_ref,
    lf_ref,
    w_hbm,
    og_hbm,
    pg_hbm,
    sg_ref,
    lg_ref,
    gath,
    wv,
    pw,
    pf,
    mixed,
    prod,
    resp,
    fmat,
    bmat,
    taps_f,
    taps_b,
    taps_ch,
    acc,
    grb,
    nxt,
    gm,
    head_out,
    head_in,
    gp1,
    lacc,
    sgc,
    xbuf,
    zbuf,
    pgv,
    local_sem,
    ring_send,
    ring_recv,
    sib_send,
    sib_recv,
    halo_send,
    halo_recv,
    x_send,
    x_recv,
    z_send,
    z_recv,
    out_sem,
):
    nx, nz, ny = dims
    n_ctx = nx * nz
    i = lax.axis_index("ctx")
    k = lax.axis_index("tp")
    x, z = lax.rem(i, nx), i // nx
    y, core = k // 2, lax.rem(k, 2)
    count = proj_hbm.shape[1]
    chan = proj_hbm.shape[2]
    model = w_hbm.shape[1]
    short = sf_ref.shape[1]
    long = lf_ref.shape[0]
    groups = lf_ref.shape[1]
    per_group = chan // groups
    lanes_n = chan // LB
    in_block = LB // per_group
    rows_chip = 2 * og_hbm.shape[0]
    half = model // 2

    right = lax.rem(y + 1, ny) * 2 + core
    left = lax.rem(y + ny - 1, ny) * 2 + core
    sibling = y * 2 + 1 - core
    following = lax.rem(i + 1, n_ctx)
    previous = lax.rem(i + n_ctx - 1, n_ctx)
    x_peers = [z * nx + lax.rem(x + d, nx) for d in range(1, nx)]
    z_peers = [lax.rem(z + d, nz) * nx + x for d in range(1, nz)]

    barrier = pltpu.get_barrier_semaphore()
    tp_greet = [right, left, sibling]
    ctx_greet = [following, previous] + x_peers + z_peers
    for other in tp_greet:
        pl.semaphore_signal(barrier, inc=1, device_id={"tp": other}, device_id_type=MESH)
    for other in ctx_greet:
        pl.semaphore_signal(barrier, inc=1, device_id={"ctx": other}, device_id_type=MESH)

    og_copy = pltpu.make_async_copy(og_hbm, gath.at[k], local_sem.at[0])
    og_copy.start()
    proj_copy = pltpu.make_async_copy(proj_hbm, pw.at[:, pl.ds(HALO, count), :], local_sem.at[1])
    proj_copy.start()
    w_copy = pltpu.make_async_copy(w_hbm, wv, local_sem.at[2])
    w_copy.start()
    og_copy.wait()
    proj_copy.wait()
    pl.semaphore_wait(barrier, len(tp_greet) + len(ctx_greet))

    steps = ny // 2

    def chunks(direction, step):
        return (0, 1) if step < steps else (direction,)

    def chip_at(direction, distance):
        if direction == 0:
            return lax.rem(y + ny - distance, ny)
        return lax.rem(y + distance, ny)

    def part(direction, distance, chunk):
        block = chip_at(direction, distance) * 2 + core
        return gath.at[block, :, pl.ds(chunk * half, half)]

    def ring(direction, step, chunk):
        ref = part(direction, step - 1, chunk)
        return pltpu.make_async_remote_copy(
            src_ref=ref,
            dst_ref=ref,
            send_sem=ring_send.at[direction, step - 1, chunk],
            recv_sem=ring_recv.at[direction, step - 1, chunk],
            device_id={"tp": right if direction == 0 else left},
            device_id_type=MESH,
        )

    def ring_arrival(direction, step, chunk):
        ref = part(direction, step, chunk)
        return pltpu.make_async_remote_copy(
            src_ref=ref,
            dst_ref=ref,
            send_sem=ring_send.at[direction, step - 1, chunk],
            recv_sem=ring_recv.at[direction, step - 1, chunk],
            device_id={"tp": right if direction == 0 else left},
            device_id_type=MESH,
        )

    def across(direction, step, chunk, own):
        block = chip_at(direction, step) * 2 + (core if own else 1 - core)
        ref = gath.at[block, :, pl.ds(chunk * half, half)]
        return pltpu.make_async_remote_copy(
            src_ref=ref,
            dst_ref=ref,
            send_sem=sib_send.at[direction, step, chunk],
            recv_sem=sib_recv.at[direction, step, chunk],
            device_id={"tp": sibling},
            device_id_type=MESH,
        )

    for chunk in range(2):
        for direction in range(2):
            if chunk in chunks(direction, 1):
                ring(direction, 1, chunk).start()
    halo = pltpu.make_async_remote_copy(
        src_ref=pw.at[:, pl.ds(count, HALO), :],
        dst_ref=pw.at[:, pl.ds(0, HALO), :],
        send_sem=halo_send.at[0],
        recv_sem=halo_recv.at[0],
        device_id={"ctx": following},
        device_id_type=MESH,
    )
    halo.start()
    for chunk in range(2):
        across(0, 0, chunk, True).start()

    def service(step, chunk):
        for direction in range(2):
            if chunk in chunks(direction, step):
                ring_arrival(direction, step, chunk).wait_recv()
                if step < steps and chunk in chunks(direction, step + 1):
                    ring(direction, step + 1, chunk).start()
                across(direction, step, chunk, True).start()

    def across_arrivals(step):
        for direction in range(2 if step > 0 else 1):
            for chunk in chunks(direction, step):
                across(direction, step, chunk, False).wait_recv()

    def build_taps():
        spread = one_hot((groups, chan), lambda r, c: c // per_group == r)
        for j in range(3):
            taps_ch[j, 0:short, :] = jnp.dot(
                sf_ref[j], spread, precision=HI, preferred_element_type=F32
            )
        lf = lf_ref[...].astype(F32)
        taps_f[...] = lax.dot_general(
            lf,
            one_hot((long, 2 * long), lambda r, c: c == long - r),
            TN,
            preferred_element_type=F32,
        )
        taps_b[...] = lax.dot_general(
            lf, one_hot((long, 2 * long), lambda r, c: c == r), TN, preferred_element_type=F32
        )

    def build_matrix(taps, matrix, start, stop):
        def body(g, carry):
            row = jnp.broadcast_to(taps[pl.ds(g, 1), :], (long, 2 * long))
            turned = pltpu.roll(row, 0, 1, stride=1, stride_axis=0)
            matrix[pl.ds(pl.multiple_of(g * long, long), long), :] = turned.astype(BF)
            return carry

        lax.fori_loop(start, stop, body, 0)

    lane_group = lax.broadcasted_iota(jnp.int32, (long, LB), 1) // per_group

    def pick(result, b):
        total = jnp.zeros((long, LB), F32)
        for g in range(in_block):
            piece = result[g * long : (g + 1) * long, b * LB : (b + 1) * LB]
            total = jnp.where(lane_group == g, piece, total)
        return total

    def lane_slice(lb):
        return pl.ds(pl.multiple_of(lb * LB, LB), LB)

    def group_rows(lb):
        return pl.ds(pl.multiple_of(lb * in_block * long, in_block * long), in_block * long)

    def widen():
        def body(j, carry):
            pf[j, HALO : HALO + count, :] = pw[j, HALO : HALO + count, :].astype(F32)
            edge = pw[j, 0:HALO, :].astype(F32)
            pf[j, 0:HALO, :] = jnp.where(i == 0, 0.0, edge)
            return carry

        lax.fori_loop(0, 3, body, 0)

    base = HALO - long

    def short_forward():
        def body(step, carry):
            j, lb = step // lanes_n, lax.rem(step, lanes_n)
            ls = lane_slice(lb)
            for blk in range(3):
                total = jnp.zeros((long, LB), F32)
                for s in range(short):
                    first = base + blk * long - s
                    total = total + taps_ch[j, s : s + 1, ls] * pf[j, first : first + long, ls]
                mixed[j, blk * long : (blk + 1) * long, ls] = total.astype(BF)
            return carry

        lax.fori_loop(0, 3 * lanes_n, body, 0)

    def long_forward():
        def body(lb, carry):
            ls = lane_slice(lb)
            value = mixed[1, :, ls].astype(F32) * mixed[2, :, ls].astype(F32)
            prod[:, ls] = value.astype(BF)
            window = jnp.concatenate([prod[0 : 2 * long, ls], prod[long : 3 * long, ls]], axis=1)
            result = jnp.dot(fmat[group_rows(lb), :], window, preferred_element_type=F32)
            for b in range(2):
                resp[b * long : (b + 1) * long, ls] = pick(result, b)
            return carry

        lax.fori_loop(0, lanes_n, body, 0)

    kc = min(1024, model)

    def project(chips):
        def body(c, carry):
            cols = pl.ds(pl.multiple_of(c * kc, kc), kc)
            xs = [gath[pl.ds(2 * chip, 2), :, cols].reshape(rows_chip, kc) for chip in chips]
            lhs = jnp.concatenate(xs, axis=0) if len(xs) > 1 else xs[0]
            return carry + lax.dot_general(lhs, wv[:, cols], NT, preferred_element_type=F32)

        zero = jnp.zeros((rows_chip * len(chips), chan), F32)
        total = lax.fori_loop(0, model // kc, body, zero)
        for q, chip in enumerate(chips):
            rows = pl.ds(pl.multiple_of(chip * rows_chip, rows_chip), rows_chip)
            acc[rows, :] = total[q * rows_chip : (q + 1) * rows_chip].astype(BF)

    def branch(chips):
        for chip in chips:
            start = chip * rows_chip
            rows = pl.ds(pl.multiple_of(start, rows_chip), rows_chip)
            own = pl.ds(pl.multiple_of(start + long, rows_chip), rows_chip)
            ob = acc[rows, :].astype(F32)
            gm[0, own, :] = (ob * resp[rows, :]).astype(BF).astype(F32)
            grb[own, :] = (ob * mixed[0, own, :].astype(F32)).astype(BF)

    build_taps()
    build_matrix(taps_f, fmat, 0, groups)
    grb[0:long, :] = jnp.zeros((long, chan), BF)
    grb[long + count :, :] = jnp.zeros((long, chan), BF)
    gm[0, 0:long, :] = jnp.zeros((long, chan), F32)
    for j in range(3):
        sgc[j, :, :] = jnp.zeros((8, chan), F32)

    if steps > 1:
        service(1, 0)
    build_matrix(taps_b, bmat, 0, groups)
    w_copy.wait()
    if steps > 1:
        service(1, 1)
        across_arrivals(0)
        across_arrivals(1)
        near = [y, chip_at(0, 1), chip_at(1, 1)]
    else:
        across_arrivals(0)
        near = [y]
    project(near)
    halo.wait_recv()
    if steps > 2:
        service(2, 0)
    widen()
    short_forward()
    if steps > 2:
        service(2, 1)
    long_forward()
    branch(near)
    for step in range(3, steps):
        service(step, 0)
        service(step, 1)
    middle = []
    for step in range(2, steps):
        across_arrivals(step)
        middle += [chip_at(0, step), chip_at(1, step)]
    if middle:
        project(middle)
        branch(middle)
    service(steps, 0)
    service(steps, 1)
    across_arrivals(steps)
    far = [chip_at(0, steps)]
    project(far)
    branch(far)

    back = pltpu.make_async_remote_copy(
        src_ref=grb.at[pl.ds(long, long), :],
        dst_ref=nxt,
        send_sem=halo_send.at[1],
        recv_sem=halo_recv.at[1],
        device_id={"ctx": previous},
        device_id_type=MESH,
    )

    def long_backward():
        def body(lb, carry):
            ls = lane_slice(lb)
            window = jnp.concatenate(
                [grb[b * long : (b + 2) * long, ls] for b in range(3)], axis=1
            )
            result = jnp.dot(bmat[group_rows(lb), :], window, preferred_element_type=F32)
            for b in range(3):
                rows = slice(b * long, (b + 1) * long)
                grad = pick(result, b)
                if b == 2:
                    gp1[:, ls] = grad
                grad = grad.astype(BF).astype(F32)
                gm[1, rows, ls] = (grad * mixed[2, rows, ls].astype(F32)).astype(BF).astype(F32)
                gm[2, rows, ls] = (grad * mixed[1, rows, ls].astype(F32)).astype(BF).astype(F32)
            return carry

        lax.fori_loop(0, lanes_n, body, 0)

    def long_taps():
        flip = one_hot((long, long), lambda r, c: r + c == long - 1).astype(BF)
        wide_group = lax.broadcasted_iota(jnp.int32, (long, 2 * LB), 1) % LB // per_group

        def body(lb, carry):
            ls = lane_slice(lb)
            grads = jnp.concatenate(
                [grb[long : 2 * long, ls], grb[2 * long : 3 * long, ls]], axis=1
            )
            grads = jnp.dot(flip, grads, preferred_element_type=F32).astype(BF)
            window = jnp.concatenate([prod[0 : 2 * long, ls], prod[long : 3 * long, ls]], axis=1)
            only = [
                jnp.where(wide_group == g, grads, jnp.zeros_like(grads)) for g in range(in_block)
            ]
            table = lax.dot_general(
                jnp.concatenate(only, axis=0), window, NT, preferred_element_type=F32
            )
            sums = []
            for g in range(in_block):
                piece = table[g * long : (g + 1) * long]
                turned = pltpu.roll(piece, 0, 1, stride=1, stride_axis=0)
                sums.append(jnp.sum(turned, axis=0, keepdims=True))
            rows = pl.ds(pl.multiple_of(lb * in_block, in_block), in_block)
            lacc[rows, :] = jnp.concatenate(sums, axis=0)
            return carry

        lax.fori_loop(0, lanes_n, body, 0)

    def short_taps():
        def body(step, carry):
            j, lb = step // lanes_n, lax.rem(step, lanes_n)
            ls = lane_slice(lb)
            for s in range(short):
                total = jnp.zeros((1, LB), F32)
                for blk in range(3):
                    first = base + blk * long - s
                    both = gm[j, blk * long : (blk + 1) * long, ls] * pf[j, first : first + long, ls]
                    total = total + jnp.sum(both, axis=0, keepdims=True)
                sgc[j, s : s + 1, ls] = total
            return carry

        lax.fori_loop(0, 3 * lanes_n, body, 0)

    back.start()
    long_backward()
    head_out[...] = gm[:, long : long + 16, :].astype(BF)
    long_taps()
    head = pltpu.make_async_remote_copy(
        src_ref=head_out,
        dst_ref=head_in,
        send_sem=halo_send.at[2],
        recv_sem=halo_recv.at[2],
        device_id={"ctx": previous},
        device_id_type=MESH,
    )
    head.start()
    short_taps()

    xbuf[x, 0:groups, :] = lacc[:, long : 2 * long]
    total = jnp.zeros((8, LB), F32)
    for j in range(3):
        place = one_hot((chan, LB), lambda r, c: c - groups * j == r // per_group)
        total = total + jnp.dot(sgc[j], place, precision=HI, preferred_element_type=F32)
    xbuf[x, groups : groups + 8, :] = total

    def exchange(buf, me, size, peers, send, recv):
        def copy(slot, d):
            return pltpu.make_async_remote_copy(
                src_ref=buf.at[slot],
                dst_ref=buf.at[slot],
                send_sem=send.at[d - 1],
                recv_sem=recv.at[slot],
                device_id={"ctx": peers[d - 1]},
                device_id_type=MESH,
            )

        return [copy(me, d) for d in range(1, size)], [
            copy(lax.rem(me + d, size), d) for d in range(1, size)
        ]

    order = lambda size: sorted(range(size - 1), key=lambda d: -min(d + 1, size - d - 1))
    x_out, x_in = exchange(xbuf, x, nx, x_peers, x_send, x_recv)
    for d in order(nx):
        x_out[d].start()

    back.wait_recv()
    last = i == n_ctx - 1

    def finish_backward():
        def body(lb, carry):
            ls = lane_slice(lb)
            window = nxt[:, ls]
            window = jnp.where(last, jnp.zeros_like(window), window)
            result = jnp.dot(
                bmat[group_rows(lb), long : 2 * long], window, preferred_element_type=F32
            )
            rows = slice(2 * long, 3 * long)
            grad = (gp1[:, ls] + pick(result, 0)).astype(BF).astype(F32)
            gm[1, rows, ls] = (grad * mixed[2, rows, ls].astype(F32)).astype(BF).astype(F32)
            gm[2, rows, ls] = (grad * mixed[1, rows, ls].astype(F32)).astype(BF).astype(F32)
            return carry

        lax.fori_loop(0, lanes_n, body, 0)

    finish_backward()
    head.wait_recv()
    ahead = head_in[...].astype(F32)
    gm[:, long + count : long + count + 16, :] = jnp.where(last, 0.0, ahead)

    def short_backward():
        def body(step, carry):
            j, lb = step // lanes_n, lax.rem(step, lanes_n)
            ls = lane_slice(lb)
            for blk in range(2):
                total = jnp.zeros((long, LB), F32)
                for s in range(short):
                    first = (blk + 1) * long + s
                    total = total + taps_ch[j, s : s + 1, ls] * gm[j, first : first + long, ls]
                pgv[j, blk * long : (blk + 1) * long, ls] = total.astype(BF)
            return carry

        lax.fori_loop(0, 3 * lanes_n, body, 0)

    for d in range(nx - 1):
        x_in[d].wait_recv()
    total = xbuf[0]
    for d in range(1, nx):
        total = total + xbuf[d]
    zbuf[z, :, :] = total
    z_out, z_in = exchange(zbuf, z, nz, z_peers, z_send, z_recv)
    short_backward()
    for d in order(nz):
        z_out[d].start()
    out_copy = pltpu.make_async_copy(pgv, pg_hbm, out_sem)
    out_copy.start()
    for d in range(nz - 1):
        z_in[d].wait_recv()
    total = zbuf[0]
    for d in range(1, nz):
        total = total + zbuf[d]
    total = total * scale
    lg_ref[...] = lax.dot_general(
        one_hot((long, long), lambda r, c: r + c == long - 1),
        total[0:groups],
        NT,
        precision=HI,
        preferred_element_type=F32,
    )
    for j in range(3):
        place = one_hot((LB, groups), lambda r, c: r - groups * j == c)
        sums = jnp.dot(total[groups : groups + 8], place, precision=HI, preferred_element_type=F32)
        sg_ref[j] = sums[0:short]

    for step in range(1, steps + 1):
        for direction in range(2):
            for chunk in chunks(direction, step):
                ring(direction, step, chunk).wait_send()
                across(direction, step, chunk, True).wait_send()
    for chunk in range(2):
        across(0, 0, chunk, True).wait_send()
    halo.wait_send()
    back.wait_send()
    head.wait_send()
    for copy in x_out + z_out:
        copy.wait_send()
    out_copy.wait()


def solution(mesh):
    n_ctx, n_tp = mesh.shape["ctx"], mesh.shape["tp"]
    nx = math.isqrt(n_ctx)
    nx = nx if nx * nx == n_ctx else n_ctx
    dims = (nx, n_ctx // nx, n_tp // 2)

    def step(projected, short_filter, long_filter, out_weight, out_grad):
        _, count, chan = projected.shape
        long, groups = long_filter.shape
        model = out_weight.shape[1]
        scale = 1.0 / math.sqrt(n_ctx * count * (chan // groups))
        steps = dims[2] // 2
        anywhere = pl.BlockSpec(memory_space=pl.ANY)
        vmem = pl.BlockSpec(memory_space=pltpu.VMEM)
        dma = pltpu.SemaphoreType.DMA
        return pl.pallas_call(
            functools.partial(kernel, dims, scale),
            name="hyena_backward",
            out_shape=(
                jax.ShapeDtypeStruct(projected.shape, BF),
                jax.ShapeDtypeStruct(short_filter.shape, F32),
                jax.ShapeDtypeStruct(long_filter.shape, F32),
            ),
            in_specs=[anywhere, vmem, vmem, anywhere, anywhere],
            out_specs=(anywhere, vmem, vmem),
            scratch_shapes=[
                pltpu.VMEM((n_tp, out_grad.shape[0], model), BF),
                pltpu.VMEM((chan, model), BF),
                pltpu.VMEM((3, HALO + count, chan), BF),
                pltpu.VMEM((3, HALO + count, chan), F32),
                pltpu.VMEM((3, long + count, chan), BF),
                pltpu.VMEM((long + count, chan), BF),
                pltpu.VMEM((count, chan), F32),
                pltpu.VMEM((groups * long, 2 * long), BF),
                pltpu.VMEM((groups * long, 2 * long), BF),
                pltpu.VMEM((groups, 2 * long), F32),
                pltpu.VMEM((groups, 2 * long), F32),
                pltpu.VMEM((3, 8, chan), F32),
                pltpu.VMEM((count, chan), BF),
                pltpu.VMEM((count + 2 * long, chan), BF),
                pltpu.VMEM((long, chan), BF),
                pltpu.VMEM((3, long + count + 16, chan), F32),
                pltpu.VMEM((3, 16, chan), BF),
                pltpu.VMEM((3, 16, chan), BF),
                pltpu.VMEM((long, chan), F32),
                pltpu.VMEM((groups, 2 * long), F32),
                pltpu.VMEM((3, 8, chan), F32),
                pltpu.VMEM((dims[0], groups + 8, long), F32),
                pltpu.VMEM((dims[1], groups + 8, long), F32),
                pltpu.VMEM((3, count, chan), BF),
                dma((3,)),
                dma((2, steps, 2)),
                dma((2, steps, 2)),
                dma((2, steps + 1, 2)),
                dma((2, steps + 1, 2)),
                dma((3,)),
                dma((3,)),
                dma((max(1, dims[0] - 1),)),
                dma((dims[0],)),
                dma((max(1, dims[1] - 1),)),
                dma((dims[1],)),
                dma,
            ],
            compiler_params=pltpu.CompilerParams(
                collective_id=0, has_side_effects=True, vmem_limit_bytes=60 * 1024 * 1024
            ),
        )(projected, short_filter, long_filter, out_weight, out_grad)

    placed = (
        P(None, "ctx", "tp"),
        P(None, None, "tp"),
        P(None, "tp"),
        P("tp", None),
        P(("ctx", "tp"), None),
    )
    return jax.shard_map(
        step,
        mesh=mesh,
        in_specs=placed,
        out_specs=(P(None, "ctx", "tp"), P(None, None, "tp"), P(None, "tp")),
        check_vma=False,
    )
```

```python
import functools
import math

import jax
import jax.numpy as jnp
from jax import lax
from jax.experimental import pallas as pl
from jax.experimental.pallas import tpu as pltpu
from jax.sharding import PartitionSpec as P

MESH = pl.DeviceIdType.MESH
BF = jnp.bfloat16
F32 = jnp.float32
HALO = 144
LB = 128
PIECES = 4
NT = (((1,), (1,)), ((), ()))
HI = lax.Precision.HIGHEST


def one_hot(shape, test):
    rows = lax.broadcasted_iota(jnp.int32, shape, 0)
    cols = lax.broadcasted_iota(jnp.int32, shape, 1)
    return jnp.where(test(rows, cols), 1.0, 0.0)


def kernel(
    dims,
    scale,
    proj_hbm,
    sf_ref,
    lf_ref,
    w_hbm,
    og_hbm,
    pg_hbm,
    sg_ref,
    lg_ref,
    gath,
    wv,
    pw,
    pf,
    mixed,
    prod,
    resp,
    fmat,
    bmat,
    taps_f,
    taps_b,
    taps_ch,
    acc,
    grb,
    nxt,
    gm,
    head_out,
    head_in,
    gp1,
    lacc,
    sgc,
    first_x,
    then_z,
    first_z,
    then_x,
    short_x,
    short_z,
    tmp,
    pgv,
    local_sem,
    ring_send,
    ring_recv,
    sib_send,
    sib_recv,
    halo_send,
    halo_recv,
    sum_send,
    sum_recv,
    out_sem,
):
    nx, nz, ny = dims
    n_ctx = nx * nz
    i = lax.axis_index("ctx")
    k = lax.axis_index("tp")
    x, z = lax.rem(i, nx), i // nx
    y, core = k // 2, lax.rem(k, 2)
    count = proj_hbm.shape[1]
    chan = proj_hbm.shape[2]
    model = w_hbm.shape[1]
    short = sf_ref.shape[1]
    groups, long = lf_ref.shape
    per_group = chan // groups
    lanes_n = chan // LB
    in_block = LB // per_group
    rows_chip = 2 * og_hbm.shape[0]
    piece = model // PIECES

    right = lax.rem(y + 1, ny) * 2 + core
    left = lax.rem(y + ny - 1, ny) * 2 + core
    sibling = y * 2 + 1 - core
    following = lax.rem(i + 1, n_ctx)
    previous = lax.rem(i + n_ctx - 1, n_ctx)
    x_peers = [z * nx + lax.rem(x + d, nx) for d in range(1, nx)]
    z_peers = [lax.rem(z + d, nz) * nx + x for d in range(1, nz)]

    barrier = pltpu.get_barrier_semaphore()
    tp_greet = [right, left, sibling]
    ctx_greet = [following, previous] + x_peers + z_peers
    for other in tp_greet:
        pl.semaphore_signal(barrier, inc=1, device_id={"tp": other}, device_id_type=MESH)
    for other in ctx_greet:
        pl.semaphore_signal(barrier, inc=1, device_id={"ctx": other}, device_id_type=MESH)

    og_copy = pltpu.make_async_copy(og_hbm, gath.at[k], local_sem.at[0])
    og_copy.start()
    proj_copy = pltpu.make_async_copy(proj_hbm, pw.at[:, pl.ds(HALO, count), :], local_sem.at[1])
    proj_copy.start()
    w_copy = pltpu.make_async_copy(w_hbm, wv, local_sem.at[2])
    w_copy.start()
    pl.semaphore_wait(barrier, len(tp_greet) + len(ctx_greet))

    steps = ny // 2

    def chunks(direction, step):
        if step < steps:
            return tuple(range(PIECES))
        return tuple(range(direction * PIECES // 2, (direction + 1) * PIECES // 2))

    def chip_at(direction, distance):
        if direction == 0:
            return lax.rem(y + ny - distance, ny)
        return lax.rem(y + distance, ny)

    def columns(chunk):
        return pl.ds(chunk * piece, piece)

    def ring(direction, step, chunk, arriving=False):
        block = chip_at(direction, step if arriving else step - 1) * 2 + core
        ref = gath.at[block, :, columns(chunk)]
        own = step == 1 and not arriving
        return pltpu.make_async_remote_copy(
            src_ref=og_hbm.at[:, columns(chunk)] if own else ref,
            dst_ref=ref,
            send_sem=ring_send.at[direction, step - 1, chunk],
            recv_sem=ring_recv.at[direction, step - 1, chunk],
            device_id={"tp": right if direction == 0 else left},
            device_id_type=MESH,
        )

    def across(direction, step, chunk, own):
        block = chip_at(direction, step) * 2 + (core if own else 1 - core)
        ref = gath.at[block, :, columns(chunk)]
        return pltpu.make_async_remote_copy(
            src_ref=og_hbm.at[:, columns(chunk)] if own and step == 0 else ref,
            dst_ref=ref,
            send_sem=sib_send.at[direction, step, chunk],
            recv_sem=sib_recv.at[direction, step, chunk],
            device_id={"tp": sibling},
            device_id_type=MESH,
        )

    for chunk in range(PIECES):
        for direction in range(2):
            if chunk in chunks(direction, 1):
                ring(direction, 1, chunk).start()
    halo = pltpu.make_async_remote_copy(
        src_ref=proj_hbm.at[:, pl.ds(count - HALO, HALO), :],
        dst_ref=pw.at[:, pl.ds(0, HALO), :],
        send_sem=halo_send.at[0],
        recv_sem=halo_recv.at[0],
        device_id={"ctx": following},
        device_id_type=MESH,
    )
    halo.start()
    for chunk in range(PIECES):
        across(0, 0, chunk, True).start()

    def service(step, which):
        for chunk in which:
            for direction in range(2):
                if chunk in chunks(direction, step):
                    ring(direction, step, chunk, True).wait_recv()
                    if step < steps and chunk in chunks(direction, step + 1):
                        ring(direction, step + 1, chunk).start()
                    across(direction, step, chunk, True).start()

    def across_arrivals(step, which=tuple(range(PIECES))):
        for direction in range(2 if step > 0 else 1):
            for chunk in chunks(direction, step):
                if chunk in which:
                    across(direction, step, chunk, False).wait_recv()

    def build_taps():
        spread = one_hot((groups, chan), lambda r, c: c // per_group == r)
        for j in range(3):
            taps_ch[j, 0:short, :] = jnp.dot(
                sf_ref[j], spread, precision=HI, preferred_element_type=F32
            )
        lf = lf_ref[...]
        backwards = one_hot((long, 2 * long), lambda r, c: c == long - r).astype(BF)
        taps_f[...] = jnp.dot(lf, backwards, preferred_element_type=F32)
        taps_b[:, 0:long] = lf.astype(F32)
        taps_b[:, long:] = jnp.zeros((groups, long), F32)

    def build_matrix(taps, matrix, start, stop):
        def body(g, carry):
            row = jnp.broadcast_to(taps[pl.ds(g, 1), :], (long, 2 * long))
            turned = pltpu.roll(row, 0, 1, stride=1, stride_axis=0)
            matrix[pl.ds(pl.multiple_of(g * long, long), long), :] = turned.astype(BF)
            return carry

        lax.fori_loop(start, stop, body, 0)

    lane_group = lax.broadcasted_iota(jnp.int32, (long, LB), 1) // per_group

    def pick(result, b):
        total = jnp.zeros((long, LB), F32)
        for g in range(in_block):
            piece = result[g * long : (g + 1) * long, b * LB : (b + 1) * LB]
            total = jnp.where(lane_group == g, piece, total)
        return total

    def lane_slice(lb):
        return pl.ds(pl.multiple_of(lb * LB, LB), LB)

    def group_rows(lb):
        return pl.ds(pl.multiple_of(lb * in_block * long, in_block * long), in_block * long)

    base = HALO - long
    far_rows = (long + count) // 8
    near_rows = count // 8

    def rows_apart(ref, j, lb, first, stride):
        return ref[j, lb, pl.ds(first, 8, stride=stride), :]

    def widen():
        def body(j, carry):
            for lb in range(lanes_n):
                ls = slice(lb * LB, (lb + 1) * LB)
                pf[j, lb, HALO : HALO + count, :] = pw[j, HALO : HALO + count, ls].astype(F32)
                edge = pw[j, 0:HALO, ls].astype(F32)
                pf[j, lb, 0:HALO, :] = jnp.where(i == 0, 0.0, edge)
            return carry

        lax.fori_loop(0, 3, body, 0)

    def short_forward():
        def body(step, carry):
            j, lb = step // lanes_n, lax.rem(step, lanes_n)
            ls = lane_slice(lb)
            taps = [jnp.broadcast_to(taps_ch[j, s : s + 1, ls], (8, LB)) for s in range(short)]
            held = [rows_apart(pf, j, lb, base - s, far_rows) for s in range(short - 1, 0, -1)]
            for q in range(far_rows):
                held.append(rows_apart(pf, j, lb, base + q, far_rows))
                total = taps[0] * held[-1]
                for s in range(1, short):
                    total = total + taps[s] * held[-1 - s]
                held = held[1:]
                mixed[j, lb, pl.ds(q, 8, stride=far_rows), :] = total.astype(BF).astype(F32)
            return carry

        lax.fori_loop(0, 3 * lanes_n, body, 0)

    def long_forward():
        def body(lb, carry):
            ls = lane_slice(lb)
            prod[:, ls] = (mixed[1, lb] * mixed[2, lb]).astype(BF)
            window = jnp.concatenate([prod[0 : 2 * long, ls], prod[long : 3 * long, ls]], axis=1)
            result = jnp.dot(fmat[group_rows(lb), :], window, preferred_element_type=F32)
            for b in range(2):
                resp[b * long : (b + 1) * long, ls] = pick(result, b)
            return carry

        lax.fori_loop(0, lanes_n, body, 0)

    kc = piece

    def project(chips, first=0, last=None):
        rows_n = rows_chip * len(chips)
        last = model // kc if last is None else last

        def body(c, carry):
            cols = pl.ds(pl.multiple_of(c * kc, kc), kc)
            xs = [gath[pl.ds(2 * chip, 2), :, cols].reshape(rows_chip, kc) for chip in chips]
            rhs = jnp.concatenate(xs, axis=0) if len(xs) > 1 else xs[0]
            return carry + lax.dot_general(wv[:, cols], rhs, NT, preferred_element_type=F32)

        total = jnp.zeros((chan, rows_n), F32)
        if last - first > 2:
            return lax.fori_loop(first, last, body, total)
        for c in range(first, last):
            total = body(c, total)
        return total

    def keep(total, chips):
        total = total.T.astype(BF)
        for q, chip in enumerate(chips):
            rows = pl.ds(pl.multiple_of(chip * rows_chip, rows_chip), rows_chip)
            acc[rows, :] = total[q * rows_chip : (q + 1) * rows_chip]

    def branch(chips):
        for chip in chips:
            start = chip * rows_chip
            rows = pl.ds(pl.multiple_of(start, rows_chip), rows_chip)
            own = pl.ds(pl.multiple_of(start + long, rows_chip), rows_chip)
            for lb in range(lanes_n):
                ls = slice(lb * LB, (lb + 1) * LB)
                ob = acc[rows, ls].astype(F32)
                gm[0, lb, own, :] = (ob * resp[rows, ls]).astype(BF).astype(F32)
                grb[own, ls] = (ob * mixed[0, lb, own, :]).astype(BF)

    low, high = tuple(range(PIECES // 2)), tuple(range(PIECES // 2, PIECES))
    build_taps()
    build_matrix(taps_f, fmat, 0, groups)
    grb[0:long, :] = jnp.zeros((long, chan), BF)
    grb[long + count :, :] = jnp.zeros((long, chan), BF)
    for j in range(3):
        sgc[j, :, :] = jnp.zeros((8, chan), F32)
    if steps > 1:
        service(1, low)
    build_matrix(taps_b, bmat, 0, groups * 3 // 4)
    if steps > 1:
        service(1, high)
    build_matrix(taps_b, bmat, groups * 3 // 4, groups)
    if steps > 2:
        service(2, low)
    proj_copy.wait()
    halo.wait_recv()
    widen()
    short_forward()
    if steps > 2:
        service(2, high)
    long_forward()
    near = [y]
    for step in range(1, steps - 1):
        near += [chip_at(0, step), chip_at(1, step)]
    og_copy.wait()
    w_copy.wait()
    for step in range(steps - 1):
        across_arrivals(step)
    if steps > 2:
        total = project(near, 0, PIECES // 2)
        service(3, low)
        keep(total + project(near, PIECES // 2, PIECES), near)
    else:
        keep(project(near), near)
    branch(near)
    if steps > 2:
        service(3, high)
    across_arrivals(steps - 1)
    far = [chip_at(0, steps - 1), chip_at(0, steps), chip_at(1, steps - 1)]
    total = jnp.zeros((chan, 3 * rows_chip), F32)
    for q in range(PIECES // 2):
        both = (q, q + PIECES // 2)
        service(steps, both)
        across_arrivals(steps, both)
        for chunk in both:
            total = total + project(far, chunk, chunk + 1)
    keep(total, far)
    branch(far)

    back = pltpu.make_async_remote_copy(
        src_ref=grb.at[pl.ds(long, long), :],
        dst_ref=nxt,
        send_sem=halo_send.at[1],
        recv_sem=halo_recv.at[1],
        device_id={"ctx": previous},
        device_id_type=MESH,
    )

    def set_products(rows, lb, grad):
        grad = grad.astype(BF).astype(F32)
        gm[1, lb, rows, :] = (grad * mixed[2, lb, rows, :]).astype(BF).astype(F32)
        gm[2, lb, rows, :] = (grad * mixed[1, lb, rows, :]).astype(BF).astype(F32)

    def long_backward(start, stop):
        def body(lb, carry):
            ls = lane_slice(lb)
            window = jnp.concatenate(
                [grb[b * long : (b + 2) * long, ls] for b in range(3)], axis=1
            )
            result = jnp.dot(bmat[group_rows(lb), :], window, preferred_element_type=F32)
            for b in range(3):
                grad = pick(result, b)
                if b == 2:
                    gp1[:, ls] = grad
                set_products(slice(b * long, (b + 1) * long), lb, grad)
            return carry

        lax.fori_loop(start, stop, body, 0)

    def long_taps():
        flip = one_hot((long, long), lambda r, c: r + c == long - 1).astype(BF)
        wide_group = lax.broadcasted_iota(jnp.int32, (long, 2 * LB), 1) % LB // per_group

        def body(lb, carry):
            ls = lane_slice(lb)
            grads = jnp.concatenate(
                [grb[long : 2 * long, ls], grb[2 * long : 3 * long, ls]], axis=1
            )
            grads = jnp.dot(flip, grads, preferred_element_type=F32).astype(BF)
            window = jnp.concatenate([prod[0 : 2 * long, ls], prod[long : 3 * long, ls]], axis=1)
            only = [
                jnp.where(wide_group == g, grads, jnp.zeros_like(grads)) for g in range(in_block)
            ]
            table = lax.dot_general(
                jnp.concatenate(only, axis=0), window, NT, preferred_element_type=F32
            )
            sums = []
            for g in range(in_block):
                piece = table[g * long : (g + 1) * long]
                turned = pltpu.roll(piece, 0, 1, stride=1, stride_axis=0)
                sums.append(jnp.sum(turned[:, long:], axis=0, keepdims=True))
            rows = pl.ds(pl.multiple_of(lb * in_block, in_block), in_block)
            lacc[rows, :] = jnp.concatenate(sums, axis=0)
            return carry

        lax.fori_loop(0, lanes_n, body, 0)

    def short_taps(streams, first, apart):
        def body(step, carry):
            j, lb = streams[0] + step // lanes_n, lax.rem(step, lanes_n)
            ls = lane_slice(lb)
            origin = base + first
            held = [rows_apart(pf, j, lb, origin - s, apart) for s in range(short - 1, 0, -1)]
            sums = [jnp.zeros((8, LB), F32)] * short
            for q in range(apart):
                held.append(rows_apart(pf, j, lb, origin + q, apart))
                grad = rows_apart(gm, j, lb, first + q, apart)
                sums = [sums[s] + grad * held[-1 - s] for s in range(short)]
                held = held[1:]
            for s in range(short):
                sgc[j, s : s + 1, ls] = jnp.sum(sums[s], axis=0, keepdims=True)
            return carry

        lax.fori_loop(0, len(streams) * lanes_n, body, 0)

    def exchange(number, buf, me, size, peers):
        def copy(slot, d):
            return pltpu.make_async_remote_copy(
                src_ref=buf.at[slot],
                dst_ref=buf.at[slot],
                send_sem=sum_send.at[number, d - 1],
                recv_sem=sum_recv.at[number, slot],
                device_id={"ctx": peers[d - 1]},
                device_id_type=MESH,
            )

        out = [copy(me, d) for d in range(1, size)]
        order = sorted(range(size - 1), key=lambda d: -min(d + 1, size - d - 1))
        return [out[d] for d in order], [copy(lax.rem(me + d, size), d) for d in range(1, size)]

    stage_ax = exchange(0, first_x, x, nx, x_peers)
    stage_az = exchange(1, then_z, z, nz, z_peers)
    stage_bz = exchange(2, first_z, z, nz, z_peers)
    stage_bx = exchange(3, then_x, x, nx, x_peers)
    stage_sx = exchange(4, short_x, x, nx, x_peers)
    stage_sz = exchange(5, short_z, z, nz, z_peers)

    def send(stage):
        for copy in stage[0]:
            copy.start()

    def gathered(stage, buf):
        for copy in stage[1]:
            copy.wait_recv()
        total = buf[0]
        for d in range(1, buf.shape[0]):
            total = total + buf[d]
        return total

    back.start()
    long_taps()
    part = groups // 2
    first_x[x, :, :] = lacc[0:part, :]
    first_z[z, :, :] = lacc[part:groups, :]
    long_backward(0, 1)
    send(stage_ax)
    send(stage_bz)
    long_backward(1, lanes_n)
    for lb in range(lanes_n):
        ls = slice(lb * LB, (lb + 1) * LB)
        head_out[:, :, ls] = gm[:, lb, long : long + 16, :].astype(BF)
    short_taps((1, 2), 0, far_rows)
    short_taps((0,), long, near_rows)
    head = pltpu.make_async_remote_copy(
        src_ref=head_out,
        dst_ref=head_in,
        send_sem=halo_send.at[2],
        recv_sem=halo_recv.at[2],
        device_id={"ctx": previous},
        device_id_type=MESH,
    )
    head.start()
    total = jnp.zeros((8, LB), F32)
    for j in range(3):
        place = one_hot((chan, LB), lambda r, c: c - groups * j == r // per_group)
        total = total + jnp.dot(sgc[j], place, precision=HI, preferred_element_type=F32)
    short_x[x, :, :] = total
    last = i == n_ctx - 1

    def finish_backward(start, stop):
        def body(lb, carry):
            ls = lane_slice(lb)
            window = nxt[:, ls]
            window = jnp.where(last, jnp.zeros_like(window), window)
            result = jnp.dot(
                bmat[group_rows(lb), long : 2 * long], window, preferred_element_type=F32
            )
            set_products(slice(2 * long, 3 * long), lb, gp1[:, ls] + pick(result, 0))
            return carry

        lax.fori_loop(start, stop, body, 0)

    back.wait_recv()
    finish_backward(0, 1)
    send(stage_sx)
    then_z[z, :, :] = gathered(stage_ax, first_x)
    then_x[x, :, :] = gathered(stage_bz, first_z)
    finish_backward(1, 2)
    send(stage_az)
    send(stage_bx)
    finish_backward(2, lanes_n)
    head.wait_recv()
    for lb in range(lanes_n):
        ls = slice(lb * LB, (lb + 1) * LB)
        ahead = jnp.where(last, 0.0, head_in[:, :, ls].astype(F32))
        gm[:, lb, long + count : long + count + 16, :] = ahead
    short_z[z, :, :] = gathered(stage_sx, short_x)

    def short_backward(start, stop):
        def body(step, carry):
            j, lb = step // lanes_n, lax.rem(step, lanes_n)
            ls = lane_slice(lb)
            taps = [jnp.broadcast_to(taps_ch[j, s : s + 1, ls], (8, LB)) for s in range(short)]
            held = [rows_apart(gm, j, lb, long + s, near_rows) for s in range(short - 1)]
            for q in range(near_rows):
                held.append(rows_apart(gm, j, lb, long + q + short - 1, near_rows))
                total = taps[0] * held[0]
                for s in range(1, short):
                    total = total + taps[s] * held[s]
                held = held[1:]
                tmp[j, lb, pl.ds(q, 8, stride=near_rows), :] = total
            pgv[j, :, ls] = tmp[j, lb].astype(BF)
            return carry

        lax.fori_loop(start, stop, body, 0)

    short_backward(0, lanes_n)
    send(stage_sz)
    short_backward(lanes_n, 3 * lanes_n)
    out_copy = pltpu.make_async_copy(pgv, pg_hbm, out_sem)
    out_copy.start()
    upper = gathered(stage_az, then_z)
    lower = gathered(stage_bx, then_x)
    total = jnp.concatenate([upper, lower], axis=0) * scale
    lg_ref[...] = jnp.dot(
        total,
        one_hot((long, long), lambda r, c: r + c == long - 1),
        precision=HI,
        preferred_element_type=F32,
    )
    total = gathered(stage_sz, short_z) * scale
    for j in range(3):
        place = one_hot((LB, groups), lambda r, c: r - groups * j == c)
        sums = jnp.dot(total, place, precision=HI, preferred_element_type=F32)
        sg_ref[j] = sums[0:short]

    for step in range(1, steps + 1):
        for direction in range(2):
            for chunk in chunks(direction, step):
                ring(direction, step, chunk).wait_send()
                across(direction, step, chunk, True).wait_send()
    for chunk in range(PIECES):
        across(0, 0, chunk, True).wait_send()
    halo.wait_send()
    back.wait_send()
    head.wait_send()
    for stage in (stage_ax, stage_az, stage_bz, stage_bx, stage_sx, stage_sz):
        for copy in stage[0]:
            copy.wait_send()
    out_copy.wait()


def solution(mesh):
    n_ctx, n_tp = mesh.shape["ctx"], mesh.shape["tp"]
    nx = math.isqrt(n_ctx)
    nx = nx if nx * nx == n_ctx else n_ctx
    dims = (nx, n_ctx // nx, n_tp // 2)

    def step(projected, short_filter, long_filter, out_weight, out_grad):
        _, count, chan = projected.shape
        long, groups = long_filter.shape
        lanes_n = chan // LB
        most = max(dims[0], dims[1])
        part = groups // 2
        model = out_weight.shape[1]
        scale = 1.0 / math.sqrt(n_ctx * count * (chan // groups))
        steps = dims[2] // 2
        anywhere = pl.BlockSpec(memory_space=pl.ANY)
        vmem = pl.BlockSpec(memory_space=pltpu.VMEM)
        dma = pltpu.SemaphoreType.DMA
        outs = pl.pallas_call(
            functools.partial(kernel, dims, scale),
            name="hyena_backward",
            out_shape=(
                jax.ShapeDtypeStruct(projected.shape, BF),
                jax.ShapeDtypeStruct(short_filter.shape, F32),
                jax.ShapeDtypeStruct((groups, long), F32),
            ),
            in_specs=[anywhere, vmem, vmem, anywhere, anywhere],
            out_specs=(anywhere, vmem, vmem),
            scratch_shapes=[
                pltpu.VMEM((n_tp, out_grad.shape[0], model), BF),
                pltpu.VMEM((chan, model), BF),
                pltpu.VMEM((3, HALO + count, chan), BF),
                pltpu.VMEM((3, lanes_n, HALO + count, LB), F32),
                pltpu.VMEM((3, lanes_n, long + count, LB), F32),
                pltpu.VMEM((long + count, chan), BF),
                pltpu.VMEM((count, chan), F32),
                pltpu.VMEM((groups * long, 2 * long), BF),
                pltpu.VMEM((groups * long, 2 * long), BF),
                pltpu.VMEM((groups, 2 * long), F32),
                pltpu.VMEM((groups, 2 * long), F32),
                pltpu.VMEM((3, 8, chan), F32),
                pltpu.VMEM((count, chan), BF),
                pltpu.VMEM((count + 2 * long, chan), BF),
                pltpu.VMEM((long, chan), BF),
                pltpu.VMEM((3, lanes_n, long + count + 16, LB), F32),
                pltpu.VMEM((3, 16, chan), BF),
                pltpu.VMEM((3, 16, chan), BF),
                pltpu.VMEM((long, chan), F32),
                pltpu.VMEM((groups, long), F32),
                pltpu.VMEM((3, 8, chan), F32),
                pltpu.VMEM((dims[0], part, long), F32),
                pltpu.VMEM((dims[1], part, long), F32),
                pltpu.VMEM((dims[1], part, long), F32),
                pltpu.VMEM((dims[0], part, long), F32),
                pltpu.VMEM((dims[0], 8, LB), F32),
                pltpu.VMEM((dims[1], 8, LB), F32),
                pltpu.VMEM((3, lanes_n, count, LB), F32),
                pltpu.VMEM((3, count, chan), BF),
                dma((3,)),
                dma((2, steps, PIECES)),
                dma((2, steps, PIECES)),
                dma((2, steps + 1, PIECES)),
                dma((2, steps + 1, PIECES)),
                dma((3,)),
                dma((3,)),
                dma((6, max(1, most - 1))),
                dma((6, most)),
                dma,
            ],
            compiler_params=pltpu.CompilerParams(
                collective_id=0, has_side_effects=True, vmem_limit_bytes=60 * 1024 * 1024
            ),
        )(projected, short_filter, long_filter.T, out_weight, out_grad)
        return outs[0], outs[1], outs[2].T

    placed = (
        P(None, "ctx", "tp"),
        P(None, None, "tp"),
        P(None, "tp"),
        P("tp", None),
        P(("ctx", "tp"), None),
    )
    return jax.shard_map(
        step,
        mesh=mesh,
        in_specs=placed,
        out_specs=(P(None, "ctx", "tp"), P(None, None, "tp"), P(None, "tp")),
        check_vma=False,
    )
```

```python
import functools
import math

import jax
import jax.numpy as jnp
from jax import lax
from jax.experimental import pallas as pl
from jax.experimental.pallas import tpu as pltpu
from jax.sharding import PartitionSpec as P

MESH = pl.DeviceIdType.MESH
BF = jnp.bfloat16
F32 = jnp.float32
HALO = 144
LB = 128
PIECES = 8
NT = (((1,), (1,)), ((), ()))
HI = lax.Precision.HIGHEST


def one_hot(shape, test):
    rows = lax.broadcasted_iota(jnp.int32, shape, 0)
    cols = lax.broadcasted_iota(jnp.int32, shape, 1)
    return jnp.where(test(rows, cols), 1.0, 0.0)


def kernel(
    dims,
    scale,
    proj_hbm,
    sf_ref,
    lf_ref,
    w_hbm,
    og_hbm,
    pg_hbm,
    sg_ref,
    lg_ref,
    gath,
    wv,
    pw,
    pf,
    mixed,
    prod,
    resp,
    fmat,
    bmat,
    taps_f,
    taps_b,
    taps_ch,
    acc,
    grb,
    nxt,
    gm,
    head_out,
    head_in,
    gp1,
    lacc,
    sgc,
    first_x,
    then_z,
    first_z,
    then_x,
    short_x,
    short_z,
    tmp,
    pgv,
    local_sem,
    ring_send,
    ring_recv,
    sib_send,
    sib_recv,
    halo_send,
    halo_recv,
    sum_send,
    sum_recv,
    out_sem,
):
    nx, nz, ny = dims
    n_ctx = nx * nz
    i = lax.axis_index("ctx")
    k = lax.axis_index("tp")
    x, z = lax.rem(i, nx), i // nx
    y, core = k // 2, lax.rem(k, 2)
    count = proj_hbm.shape[1]
    chan = proj_hbm.shape[2]
    model = w_hbm.shape[1]
    short = sf_ref.shape[1]
    groups, long = lf_ref.shape
    per_group = chan // groups
    lanes_n = chan // LB
    in_block = LB // per_group
    rows_chip = 2 * og_hbm.shape[0]
    piece = model // PIECES

    right = lax.rem(y + 1, ny) * 2 + core
    left = lax.rem(y + ny - 1, ny) * 2 + core
    sibling = y * 2 + 1 - core
    following = lax.rem(i + 1, n_ctx)
    previous = lax.rem(i + n_ctx - 1, n_ctx)
    x_peers = [z * nx + lax.rem(x + d, nx) for d in range(1, nx)]
    z_peers = [lax.rem(z + d, nz) * nx + x for d in range(1, nz)]

    barrier = pltpu.get_barrier_semaphore()
    tp_greet = [right, left, sibling]
    ctx_greet = [following, previous] + x_peers + z_peers
    for other in tp_greet:
        pl.semaphore_signal(barrier, inc=1, device_id={"tp": other}, device_id_type=MESH)
    for other in ctx_greet:
        pl.semaphore_signal(barrier, inc=1, device_id={"ctx": other}, device_id_type=MESH)

    og_copy = pltpu.make_async_copy(og_hbm, gath.at[k], local_sem.at[0])
    og_copy.start()
    proj_copy = pltpu.make_async_copy(proj_hbm, pw.at[:, pl.ds(HALO, count), :], local_sem.at[1])
    proj_copy.start()
    w_copy = pltpu.make_async_copy(w_hbm, wv, local_sem.at[2])
    w_copy.start()
    pl.semaphore_wait(barrier, len(tp_greet) + len(ctx_greet))

    steps = ny // 2

    def chunks(direction, step):
        if step < steps:
            return tuple(range(PIECES))
        return tuple(range(direction * PIECES // 2, (direction + 1) * PIECES // 2))

    def chip_at(direction, distance):
        if direction == 0:
            return lax.rem(y + ny - distance, ny)
        return lax.rem(y + distance, ny)

    def columns(chunk):
        return pl.ds(chunk * piece, piece)

    def ring(direction, step, chunk, arriving=False):
        block = chip_at(direction, step if arriving else step - 1) * 2 + core
        ref = gath.at[block, :, columns(chunk)]
        own = step == 1 and not arriving
        return pltpu.make_async_remote_copy(
            src_ref=og_hbm.at[:, columns(chunk)] if own else ref,
            dst_ref=ref,
            send_sem=ring_send.at[direction, step - 1, chunk],
            recv_sem=ring_recv.at[direction, step - 1, chunk],
            device_id={"tp": right if direction == 0 else left},
            device_id_type=MESH,
        )

    def across(direction, step, chunk, own):
        block = chip_at(direction, step) * 2 + (core if own else 1 - core)
        ref = gath.at[block, :, columns(chunk)]
        return pltpu.make_async_remote_copy(
            src_ref=og_hbm.at[:, columns(chunk)] if own and step == 0 else ref,
            dst_ref=ref,
            send_sem=sib_send.at[direction, step, chunk],
            recv_sem=sib_recv.at[direction, step, chunk],
            device_id={"tp": sibling},
            device_id_type=MESH,
        )

    for chunk in range(PIECES):
        for direction in range(2):
            if chunk in chunks(direction, 1):
                ring(direction, 1, chunk).start()
    halo = pltpu.make_async_remote_copy(
        src_ref=proj_hbm.at[:, pl.ds(count - HALO, HALO), :],
        dst_ref=pw.at[:, pl.ds(0, HALO), :],
        send_sem=halo_send.at[0],
        recv_sem=halo_recv.at[0],
        device_id={"ctx": following},
        device_id_type=MESH,
    )
    halo.start()
    for chunk in range(PIECES):
        across(0, 0, chunk, True).start()

    def service(step, which):
        for chunk in which:
            for direction in range(2):
                if chunk in chunks(direction, step):
                    ring(direction, step, chunk, True).wait_recv()
                    if step < steps and chunk in chunks(direction, step + 1):
                        ring(direction, step + 1, chunk).start()
                    across(direction, step, chunk, True).start()

    def across_arrivals(step, which=tuple(range(PIECES))):
        for direction in range(2 if step > 0 else 1):
            for chunk in chunks(direction, step):
                if chunk in which:
                    across(direction, step, chunk, False).wait_recv()

    def build_taps():
        spread = one_hot((groups, chan), lambda r, c: c // per_group == r)
        for j in range(3):
            taps_ch[j, 0:short, :] = jnp.dot(
                sf_ref[j], spread, precision=HI, preferred_element_type=F32
            )
        lf = lf_ref[...]
        backwards = one_hot((long, 2 * long), lambda r, c: c == long - r).astype(BF)
        taps_f[...] = jnp.dot(lf, backwards, preferred_element_type=F32)
        taps_b[:, 0:long] = lf.astype(F32)
        taps_b[:, long:] = jnp.zeros((groups, long), F32)

    def build_matrix(taps, matrix, start, stop):
        def body(g, carry):
            row = jnp.broadcast_to(taps[pl.ds(g, 1), :], (long, 2 * long))
            turned = pltpu.roll(row, 0, 1, stride=1, stride_axis=0)
            matrix[pl.ds(pl.multiple_of(g * long, long), long), :] = turned.astype(BF)
            return carry

        lax.fori_loop(start, stop, body, 0)

    lane_group = lax.broadcasted_iota(jnp.int32, (long, LB), 1) // per_group

    def pick(result, b):
        total = jnp.zeros((long, LB), F32)
        for g in range(in_block):
            piece = result[g * long : (g + 1) * long, b * LB : (b + 1) * LB]
            total = jnp.where(lane_group == g, piece, total)
        return total

    def lane_slice(lb):
        return pl.ds(lb * LB if isinstance(lb, int) else pl.multiple_of(lb * LB, LB), LB)

    def group_rows(lb):
        size = in_block * long
        return pl.ds(lb * size if isinstance(lb, int) else pl.multiple_of(lb * size, size), size)

    base = HALO - long
    far_rows = (long + count) // 8
    near_rows = count // 8

    def rows_apart(ref, j, lb, first, stride):
        return ref[j, lb, pl.ds(first, 8, stride=stride), :]

    def widen():
        def body(j, carry):
            for lb in range(lanes_n):
                ls = slice(lb * LB, (lb + 1) * LB)
                pf[j, lb, HALO : HALO + count, :] = pw[j, HALO : HALO + count, ls].astype(F32)
                edge = pw[j, 0:HALO, ls].astype(F32)
                pf[j, lb, 0:HALO, :] = jnp.where(i == 0, 0.0, edge)
            return carry

        lax.fori_loop(0, 3, body, 0)

    def short_forward():
        def body(step, carry):
            j, lb = step // lanes_n, lax.rem(step, lanes_n)
            ls = lane_slice(lb)
            taps = [jnp.broadcast_to(taps_ch[j, s : s + 1, ls], (8, LB)) for s in range(short)]
            held = [rows_apart(pf, j, lb, base - s, far_rows) for s in range(short - 1, 0, -1)]
            for q in range(far_rows):
                held.append(rows_apart(pf, j, lb, base + q, far_rows))
                total = taps[0] * held[-1]
                for s in range(1, short):
                    total = total + taps[s] * held[-1 - s]
                held = held[1:]
                mixed[j, lb, pl.ds(q, 8, stride=far_rows), :] = total.astype(BF).astype(F32)
            return carry

        lax.fori_loop(0, 3 * lanes_n, body, 0)

    def long_forward():
        def body(lb, carry):
            ls = lane_slice(lb)
            prod[:, ls] = (mixed[1, lb] * mixed[2, lb]).astype(BF)
            window = jnp.concatenate([prod[0 : 2 * long, ls], prod[long : 3 * long, ls]], axis=1)
            result = jnp.dot(fmat[group_rows(lb), :], window, preferred_element_type=F32)
            for b in range(2):
                resp[b * long : (b + 1) * long, ls] = pick(result, b)
            return carry

        lax.fori_loop(0, lanes_n, body, 0)

    kc = 2 * piece

    def project(chips, first, size):
        cols = pl.ds(first, size)
        xs = [gath[pl.ds(2 * chip, 2), :, cols].reshape(rows_chip, size) for chip in chips]
        rhs = jnp.concatenate(xs, axis=0) if len(xs) > 1 else xs[0]
        return lax.dot_general(wv[:, cols], rhs, NT, preferred_element_type=F32)

    def project_range(chips, first, last, total):
        def body(c, carry):
            return carry + project(chips, pl.multiple_of(c * kc, kc), kc)

        return lax.fori_loop(first * piece // kc, last * piece // kc, body, total)

    def keep(total, chips):
        total = total.T.astype(BF)
        for q, chip in enumerate(chips):
            rows = pl.ds(pl.multiple_of(chip * rows_chip, rows_chip), rows_chip)
            acc[rows, :] = total[q * rows_chip : (q + 1) * rows_chip]

    def branch(chips):
        for chip in chips:
            start = chip * rows_chip
            rows = pl.ds(pl.multiple_of(start, rows_chip), rows_chip)
            own = pl.ds(pl.multiple_of(start + long, rows_chip), rows_chip)
            for lb in range(lanes_n):
                ls = slice(lb * LB, (lb + 1) * LB)
                ob = acc[rows, ls].astype(F32)
                gm[0, lb, own, :] = (ob * resp[rows, ls]).astype(BF).astype(F32)
                grb[own, ls] = (ob * mixed[0, lb, own, :]).astype(BF)

    low, high = tuple(range(PIECES // 2)), tuple(range(PIECES // 2, PIECES))
    build_taps()
    build_matrix(taps_f, fmat, 0, groups)
    grb[0:long, :] = jnp.zeros((long, chan), BF)
    grb[long + count :, :] = jnp.zeros((long, chan), BF)
    for j in range(3):
        sgc[j, :, :] = jnp.zeros((8, chan), F32)
    if steps > 1:
        service(1, low)
    build_matrix(taps_b, bmat, 0, groups * 3 // 4)
    if steps > 1:
        service(1, high)
    build_matrix(taps_b, bmat, groups * 3 // 4, groups)
    if steps > 2:
        service(2, low)
        service(2, high)
    proj_copy.wait()
    halo.wait_recv()
    widen()
    short_forward()
    if steps > 2:
        service(3, low)
    long_forward()
    near = [y]
    for step in range(1, steps - 1):
        near += [chip_at(0, step), chip_at(1, step)]
    og_copy.wait()
    w_copy.wait()
    for step in range(steps - 1):
        across_arrivals(step)
    total = jnp.zeros((chan, len(near) * rows_chip), F32)
    total = project_range(near, 0, PIECES // 2, total)
    if steps > 2:
        service(3, high)
    total = project_range(near, PIECES // 2, PIECES, total)
    keep(total, near)
    branch(near)
    far = [chip_at(0, steps - 1), chip_at(0, steps), chip_at(1, steps - 1)]
    total = jnp.zeros((chan, 3 * rows_chip), F32)
    across_arrivals(steps - 1)
    for q in range(PIECES // 2):
        both = (q, q + PIECES // 2)
        service(steps, both)
        across_arrivals(steps, both)
        for chunk in both:
            total = total + project(far, chunk * piece, piece)
    keep(total, far)
    branch(far)

    back = pltpu.make_async_remote_copy(
        src_ref=grb.at[pl.ds(long, long), :],
        dst_ref=nxt,
        send_sem=halo_send.at[1],
        recv_sem=halo_recv.at[1],
        device_id={"ctx": previous},
        device_id_type=MESH,
    )

    def set_products(rows, lb, grad):
        grad = grad.astype(BF).astype(F32)
        gm[1, lb, rows, :] = (grad * mixed[2, lb, rows, :]).astype(BF).astype(F32)
        gm[2, lb, rows, :] = (grad * mixed[1, lb, rows, :]).astype(BF).astype(F32)

    def long_backward(lb):
        ls = lane_slice(lb)
        window = jnp.concatenate([grb[b * long : (b + 2) * long, ls] for b in range(3)], axis=1)
        result = jnp.dot(bmat[group_rows(lb), :], window, preferred_element_type=F32)
        for b in range(3):
            grad = pick(result, b)
            if b == 2:
                gp1[:, ls] = grad
            set_products(slice(b * long, (b + 1) * long), lb, grad)

    def short_taps(j, lb, first, apart):
        ls = lane_slice(lb)
        origin = base + first
        held = [rows_apart(pf, j, lb, origin - s, apart) for s in range(short - 1, 0, -1)]
        sums = [jnp.zeros((8, LB), F32)] * short
        for q in range(apart):
            held.append(rows_apart(pf, j, lb, origin + q, apart))
            grad = rows_apart(gm, j, lb, first + q, apart)
            sums = [sums[s] + grad * held[-1 - s] for s in range(short)]
            held = held[1:]
        for s in range(short):
            sgc[j, s : s + 1, ls] = jnp.sum(sums[s], axis=0, keepdims=True)

    def long_taps():
        flip = one_hot((long, long), lambda r, c: r + c == long - 1).astype(BF)
        wide_group = lax.broadcasted_iota(jnp.int32, (long, 2 * LB), 1) % LB // per_group

        def body(lb, carry):
            ls = lane_slice(lb)
            grads = jnp.concatenate(
                [grb[long : 2 * long, ls], grb[2 * long : 3 * long, ls]], axis=1
            )
            grads = jnp.dot(flip, grads, preferred_element_type=F32).astype(BF)
            window = jnp.concatenate([prod[0 : 2 * long, ls], prod[long : 3 * long, ls]], axis=1)
            only = [
                jnp.where(wide_group == g, grads, jnp.zeros_like(grads)) for g in range(in_block)
            ]
            table = lax.dot_general(
                jnp.concatenate(only, axis=0), window, NT, preferred_element_type=F32
            )
            sums = []
            for g in range(in_block):
                piece = table[g * long : (g + 1) * long]
                turned = pltpu.roll(piece, 0, 1, stride=1, stride_axis=0)
                sums.append(jnp.sum(turned[:, long:], axis=0, keepdims=True))
            rows = pl.ds(pl.multiple_of(lb * in_block, in_block), in_block)
            lacc[rows, :] = jnp.concatenate(sums, axis=0)
            short_taps(0, lb, long, near_rows)
            return carry

        lax.fori_loop(0, lanes_n, body, 0)

    def exchange(number, buf, me, size, peers):
        def copy(slot, d):
            return pltpu.make_async_remote_copy(
                src_ref=buf.at[slot],
                dst_ref=buf.at[slot],
                send_sem=sum_send.at[number, d - 1],
                recv_sem=sum_recv.at[number, slot],
                device_id={"ctx": peers[d - 1]},
                device_id_type=MESH,
            )

        out = [copy(me, d) for d in range(1, size)]
        order = sorted(range(size - 1), key=lambda d: -min(d + 1, size - d - 1))
        return [out[d] for d in order], [copy(lax.rem(me + d, size), d) for d in range(1, size)]

    stage_ax = exchange(0, first_x, x, nx, x_peers)
    stage_az = exchange(1, then_z, z, nz, z_peers)
    stage_bz = exchange(2, first_z, z, nz, z_peers)
    stage_bx = exchange(3, then_x, x, nx, x_peers)
    stage_sx = exchange(4, short_x, x, nx, x_peers)
    stage_sz = exchange(5, short_z, z, nz, z_peers)

    def send(stage):
        for copy in stage[0]:
            copy.start()

    def gathered(stage, buf):
        for copy in stage[1]:
            copy.wait_recv()
        total = buf[0]
        for d in range(1, buf.shape[0]):
            total = total + buf[d]
        return total

    def backward_and_taps():
        def body(lb, carry):
            long_backward(lb)
            short_taps(1, lb - 1, 0, far_rows)
            short_taps(2, lb - 1, 0, far_rows)
            return carry

        lax.fori_loop(1, lanes_n, body, 0)
        short_taps(1, lanes_n - 1, 0, far_rows)
        short_taps(2, lanes_n - 1, 0, far_rows)

    back.start()
    long_taps()
    part = groups // 2
    first_x[x, :, :] = lacc[0:part, :]
    first_z[z, :, :] = lacc[part:groups, :]
    long_backward(0)
    send(stage_ax)
    send(stage_bz)
    backward_and_taps()
    for lb in range(lanes_n):
        ls = slice(lb * LB, (lb + 1) * LB)
        head_out[:, :, ls] = gm[:, lb, long : long + 16, :].astype(BF)
    head = pltpu.make_async_remote_copy(
        src_ref=head_out,
        dst_ref=head_in,
        send_sem=halo_send.at[2],
        recv_sem=halo_recv.at[2],
        device_id={"ctx": previous},
        device_id_type=MESH,
    )
    head.start()
    total = jnp.zeros((8, LB), F32)
    for j in range(3):
        place = one_hot((chan, LB), lambda r, c: c - groups * j == r // per_group)
        total = total + jnp.dot(sgc[j], place, precision=HI, preferred_element_type=F32)
    short_x[x, :, :] = total
    last = i == n_ctx - 1

    def finish_backward(start, stop):
        def body(lb, carry):
            ls = lane_slice(lb)
            window = nxt[:, ls]
            window = jnp.where(last, jnp.zeros_like(window), window)
            result = jnp.dot(
                bmat[group_rows(lb), long : 2 * long], window, preferred_element_type=F32
            )
            set_products(slice(2 * long, 3 * long), lb, gp1[:, ls] + pick(result, 0))
            return carry

        lax.fori_loop(start, stop, body, 0)

    back.wait_recv()
    finish_backward(0, 1)
    send(stage_sx)
    then_z[z, :, :] = gathered(stage_ax, first_x)
    then_x[x, :, :] = gathered(stage_bz, first_z)
    finish_backward(1, 2)
    send(stage_az)
    send(stage_bx)
    finish_backward(2, lanes_n)
    head.wait_recv()
    for lb in range(lanes_n):
        ls = slice(lb * LB, (lb + 1) * LB)
        ahead = jnp.where(last, 0.0, head_in[:, :, ls].astype(F32))
        gm[:, lb, long + count : long + count + 16, :] = ahead
    short_z[z, :, :] = gathered(stage_sx, short_x)

    def short_backward(start, stop):
        def body(step, carry):
            j, lb = step // lanes_n, lax.rem(step, lanes_n)
            ls = lane_slice(lb)
            taps = [jnp.broadcast_to(taps_ch[j, s : s + 1, ls], (8, LB)) for s in range(short)]
            held = [rows_apart(gm, j, lb, long + s, near_rows) for s in range(short - 1)]
            for q in range(near_rows):
                held.append(rows_apart(gm, j, lb, long + q + short - 1, near_rows))
                total = taps[0] * held[0]
                for s in range(1, short):
                    total = total + taps[s] * held[s]
                held = held[1:]
                tmp[j, lb, pl.ds(q, 8, stride=near_rows), :] = total
            pgv[j, :, ls] = tmp[j, lb].astype(BF)
            return carry

        lax.fori_loop(start, stop, body, 0)

    short_backward(0, lanes_n)
    send(stage_sz)
    short_backward(lanes_n, 3 * lanes_n)
    out_copy = pltpu.make_async_copy(pgv, pg_hbm, out_sem)
    out_copy.start()
    upper = gathered(stage_az, then_z)
    lower = gathered(stage_bx, then_x)
    total = jnp.concatenate([upper, lower], axis=0) * scale
    lg_ref[...] = jnp.dot(
        total,
        one_hot((long, long), lambda r, c: r + c == long - 1),
        precision=HI,
        preferred_element_type=F32,
    )
    total = gathered(stage_sz, short_z) * scale
    for j in range(3):
        place = one_hot((LB, groups), lambda r, c: r - groups * j == c)
        sums = jnp.dot(total, place, precision=HI, preferred_element_type=F32)
        sg_ref[j] = sums[0:short]

    for step in range(1, steps + 1):
        for direction in range(2):
            for chunk in chunks(direction, step):
                ring(direction, step, chunk).wait_send()
                across(direction, step, chunk, True).wait_send()
    for chunk in range(PIECES):
        across(0, 0, chunk, True).wait_send()
    halo.wait_send()
    back.wait_send()
    head.wait_send()
    for stage in (stage_ax, stage_az, stage_bz, stage_bx, stage_sx, stage_sz):
        for copy in stage[0]:
            copy.wait_send()
    out_copy.wait()


def hand_over(pg_in, sg_in, lg_in, pg_out, sg_out, lg_out, pg, sg, lg, sem_in, sem_out):
    moves = [(sg_in, sg, sg_out), (lg_in, lg, lg_out)]
    for j in range(3):
        moves.append((pg_in.at[j], pg.at[j], pg_out.at[j]))
    loads = [pltpu.make_async_copy(m[0], m[1], sem_in.at[n]) for n, m in enumerate(moves)]
    stores = [pltpu.make_async_copy(m[1], m[2], sem_out.at[n]) for n, m in enumerate(moves)]
    for copy in loads:
        copy.start()
    for load, store in zip(loads, stores):
        load.wait()
        store.start()
    for copy in stores:
        copy.wait()


def solution(mesh):
    n_ctx, n_tp = mesh.shape["ctx"], mesh.shape["tp"]
    nx = math.isqrt(n_ctx)
    nx = nx if nx * nx == n_ctx else n_ctx
    dims = (nx, n_ctx // nx, n_tp // 2)

    def step(projected, short_filter, long_filter, out_weight, out_grad):
        _, count, chan = projected.shape
        long, groups = long_filter.shape
        lanes_n = chan // LB
        most = max(dims[0], dims[1])
        part = groups // 2
        model = out_weight.shape[1]
        scale = 1.0 / math.sqrt(n_ctx * count * (chan // groups))
        steps = dims[2] // 2
        anywhere = pl.BlockSpec(memory_space=pl.ANY)
        vmem = pl.BlockSpec(memory_space=pltpu.VMEM)
        dma = pltpu.SemaphoreType.DMA
        outs = pl.pallas_call(
            functools.partial(kernel, dims, scale),
            name="hyena_backward",
            out_shape=(
                jax.ShapeDtypeStruct(projected.shape, BF),
                jax.ShapeDtypeStruct(short_filter.shape, F32),
                jax.ShapeDtypeStruct((groups, long), F32),
            ),
            in_specs=[anywhere, vmem, vmem, anywhere, anywhere],
            out_specs=(anywhere, vmem, vmem),
            scratch_shapes=[
                pltpu.VMEM((n_tp, out_grad.shape[0], model), BF),
                pltpu.VMEM((chan, model), BF),
                pltpu.VMEM((3, HALO + count, chan), BF),
                pltpu.VMEM((3, lanes_n, HALO + count, LB), F32),
                pltpu.VMEM((3, lanes_n, long + count, LB), F32),
                pltpu.VMEM((long + count, chan), BF),
                pltpu.VMEM((count, chan), F32),
                pltpu.VMEM((groups * long, 2 * long), BF),
                pltpu.VMEM((groups * long, 2 * long), BF),
                pltpu.VMEM((groups, 2 * long), F32),
                pltpu.VMEM((groups, 2 * long), F32),
                pltpu.VMEM((3, 8, chan), F32),
                pltpu.VMEM((count, chan), BF),
                pltpu.VMEM((count + 2 * long, chan), BF),
                pltpu.VMEM((long, chan), BF),
                pltpu.VMEM((3, lanes_n, long + count + 16, LB), F32),
                pltpu.VMEM((3, 16, chan), BF),
                pltpu.VMEM((3, 16, chan), BF),
                pltpu.VMEM((long, chan), F32),
                pltpu.VMEM((groups, long), F32),
                pltpu.VMEM((3, 8, chan), F32),
                pltpu.VMEM((dims[0], part, long), F32),
                pltpu.VMEM((dims[1], part, long), F32),
                pltpu.VMEM((dims[1], part, long), F32),
                pltpu.VMEM((dims[0], part, long), F32),
                pltpu.VMEM((dims[0], 8, LB), F32),
                pltpu.VMEM((dims[1], 8, LB), F32),
                pltpu.VMEM((3, lanes_n, count, LB), F32),
                pltpu.VMEM((3, count, chan), BF),
                dma((3,)),
                dma((2, steps, PIECES)),
                dma((2, steps, PIECES)),
                dma((2, steps + 1, PIECES)),
                dma((2, steps + 1, PIECES)),
                dma((3,)),
                dma((3,)),
                dma((6, max(1, most - 1))),
                dma((6, most)),
                dma,
            ],
            compiler_params=pltpu.CompilerParams(
                collective_id=0, has_side_effects=True, vmem_limit_bytes=60 * 1024 * 1024
            ),
        )(projected, short_filter, long_filter.T, out_weight, out_grad)
        outs = pl.pallas_call(
            hand_over,
            name="hand_over",
            out_shape=tuple(jax.ShapeDtypeStruct(o.shape, o.dtype) for o in outs),
            in_specs=[anywhere] * 3,
            out_specs=(anywhere,) * 3,
            scratch_shapes=[pltpu.VMEM(o.shape, o.dtype) for o in outs] + [dma((5,)), dma((5,))],
        )(*outs)
        return outs[0], outs[1], outs[2].T

    placed = (
        P(None, "ctx", "tp"),
        P(None, None, "tp"),
        P(None, "tp"),
        P("tp", None),
        P(("ctx", "tp"), None),
    )
    return jax.shard_map(
        step,
        mesh=mesh,
        in_specs=placed,
        out_specs=(P(None, "ctx", "tp"), P(None, None, "tp"), P(None, "tp")),
        check_vma=False,
    )
```

```python
import functools
import math

import jax
import jax.numpy as jnp
from jax import lax
from jax.experimental import pallas as pl
from jax.experimental.pallas import tpu as pltpu
from jax.sharding import PartitionSpec as P

MESH = pl.DeviceIdType.MESH
BF = jnp.bfloat16
F32 = jnp.float32
HALO = 144
LB = 128
PIECES = 4
NT = (((1,), (1,)), ((), ()))
HI = lax.Precision.HIGHEST


def one_hot(shape, test):
    rows = lax.broadcasted_iota(jnp.int32, shape, 0)
    cols = lax.broadcasted_iota(jnp.int32, shape, 1)
    return jnp.where(test(rows, cols), 1.0, 0.0)


def kernel(
    dims,
    scale,
    proj_hbm,
    sf_ref,
    lf_ref,
    w_hbm,
    og_hbm,
    pg_hbm,
    sg_ref,
    lg_ref,
    gath,
    wv,
    pw,
    pf,
    mixed,
    prod,
    resp,
    fmat,
    bmat,
    taps_f,
    taps_b,
    taps_ch,
    acc,
    grb,
    nxt,
    gm,
    head_out,
    head_in,
    gp1,
    lacc,
    sgc,
    first_x,
    then_z,
    first_z,
    then_x,
    short_x,
    short_z,
    tmp,
    pgv,
    local_sem,
    ring_send,
    ring_recv,
    sib_send,
    sib_recv,
    halo_send,
    halo_recv,
    sum_send,
    sum_recv,
    out_sem,
):
    nx, nz, ny = dims
    n_ctx = nx * nz
    i = lax.axis_index("ctx")
    k = lax.axis_index("tp")
    x, z = lax.rem(i, nx), i // nx
    y, core = k // 2, lax.rem(k, 2)
    count = proj_hbm.shape[1]
    chan = proj_hbm.shape[2]
    model = w_hbm.shape[1]
    short = sf_ref.shape[1]
    groups, long = lf_ref.shape
    per_group = chan // groups
    lanes_n = chan // LB
    in_block = LB // per_group
    rows_chip = 2 * og_hbm.shape[0]
    piece = model // PIECES

    right = lax.rem(y + 1, ny) * 2 + core
    left = lax.rem(y + ny - 1, ny) * 2 + core
    sibling = y * 2 + 1 - core
    following = lax.rem(i + 1, n_ctx)
    previous = lax.rem(i + n_ctx - 1, n_ctx)
    x_peers = [z * nx + lax.rem(x + d, nx) for d in range(1, nx)]
    z_peers = [lax.rem(z + d, nz) * nx + x for d in range(1, nz)]

    barrier = pltpu.get_barrier_semaphore()
    tp_greet = [right, left, sibling]
    ctx_greet = [following, previous] + x_peers + z_peers
    for other in tp_greet:
        pl.semaphore_signal(barrier, inc=1, device_id={"tp": other}, device_id_type=MESH)
    for other in ctx_greet:
        pl.semaphore_signal(barrier, inc=1, device_id={"ctx": other}, device_id_type=MESH)

    og_copy = pltpu.make_async_copy(og_hbm, gath.at[k], local_sem.at[0])
    og_copy.start()
    proj_copy = pltpu.make_async_copy(proj_hbm, pw.at[:, pl.ds(HALO, count), :], local_sem.at[1])
    proj_copy.start()
    w_copy = pltpu.make_async_copy(w_hbm, wv, local_sem.at[2])
    w_copy.start()
    pl.semaphore_wait(barrier, len(tp_greet) + len(ctx_greet))

    steps = ny // 2

    def chunks(direction, step):
        if step < steps:
            return tuple(range(PIECES))
        return tuple(range(direction * PIECES // 2, (direction + 1) * PIECES // 2))

    def chip_at(direction, distance):
        if direction == 0:
            return lax.rem(y + ny - distance, ny)
        return lax.rem(y + distance, ny)

    def columns(chunk):
        return pl.ds(chunk * piece, piece)

    def ring(direction, step, chunk, arriving=False):
        block = chip_at(direction, step if arriving else step - 1) * 2 + core
        ref = gath.at[block, :, columns(chunk)]
        own = step == 1 and not arriving
        return pltpu.make_async_remote_copy(
            src_ref=og_hbm.at[:, columns(chunk)] if own else ref,
            dst_ref=ref,
            send_sem=ring_send.at[direction, step - 1, chunk],
            recv_sem=ring_recv.at[direction, step - 1, chunk],
            device_id={"tp": right if direction == 0 else left},
            device_id_type=MESH,
        )

    def across(direction, step, chunk, own):
        block = chip_at(direction, step) * 2 + (core if own else 1 - core)
        ref = gath.at[block, :, columns(chunk)]
        return pltpu.make_async_remote_copy(
            src_ref=og_hbm.at[:, columns(chunk)] if own and step == 0 else ref,
            dst_ref=ref,
            send_sem=sib_send.at[direction, step, chunk],
            recv_sem=sib_recv.at[direction, step, chunk],
            device_id={"tp": sibling},
            device_id_type=MESH,
        )

    for chunk in range(PIECES):
        for direction in range(2):
            if chunk in chunks(direction, 1):
                ring(direction, 1, chunk).start()
    halo = pltpu.make_async_remote_copy(
        src_ref=proj_hbm.at[:, pl.ds(count - HALO, HALO), :],
        dst_ref=pw.at[:, pl.ds(0, HALO), :],
        send_sem=halo_send.at[0],
        recv_sem=halo_recv.at[0],
        device_id={"ctx": following},
        device_id_type=MESH,
    )
    halo.start()
    for chunk in range(PIECES):
        across(0, 0, chunk, True).start()

    def service(step, which):
        for chunk in which:
            for direction in range(2):
                if chunk in chunks(direction, step):
                    ring(direction, step, chunk, True).wait_recv()
                    if step < steps and chunk in chunks(direction, step + 1):
                        ring(direction, step + 1, chunk).start()
                    across(direction, step, chunk, True).start()

    def across_arrivals(step, which=tuple(range(PIECES))):
        for direction in range(2 if step > 0 else 1):
            for chunk in chunks(direction, step):
                if chunk in which:
                    across(direction, step, chunk, False).wait_recv()

    def build_taps():
        spread = one_hot((groups, chan), lambda r, c: c // per_group == r)
        for j in range(3):
            taps_ch[j, 0:short, :] = jnp.dot(
                sf_ref[j], spread, precision=HI, preferred_element_type=F32
            )
        lf = lf_ref[...]
        backwards = one_hot((long, 2 * long), lambda r, c: c == long - r).astype(BF)
        taps_f[...] = jnp.dot(lf, backwards, preferred_element_type=F32)
        taps_b[:, 0:long] = lf.astype(F32)
        taps_b[:, long:] = jnp.zeros((groups, long), F32)

    def build_matrix(taps, matrix, start, stop):
        def body(g, carry):
            row = jnp.broadcast_to(taps[pl.ds(g, 1), :], (long, 2 * long))
            turned = pltpu.roll(row, 0, 1, stride=1, stride_axis=0)
            matrix[pl.ds(pl.multiple_of(g * long, long), long), :] = turned.astype(BF)
            return carry

        lax.fori_loop(start, stop, body, 0)

    lane_group = lax.broadcasted_iota(jnp.int32, (long, LB), 1) // per_group

    def pick(result, b):
        total = jnp.zeros((long, LB), F32)
        for g in range(in_block):
            piece = result[g * long : (g + 1) * long, b * LB : (b + 1) * LB]
            total = jnp.where(lane_group == g, piece, total)
        return total

    def lane_slice(lb):
        return pl.ds(lb * LB if isinstance(lb, int) else pl.multiple_of(lb * LB, LB), LB)

    def group_rows(lb):
        size = in_block * long
        return pl.ds(lb * size if isinstance(lb, int) else pl.multiple_of(lb * size, size), size)

    base = HALO - long
    far_rows = (long + count) // 8
    near_rows = count // 8

    def rows_apart(ref, j, lb, first, stride):
        return ref[j, lb, pl.ds(first, 8, stride=stride), :]

    def widen():
        def body(j, carry):
            for lb in range(lanes_n):
                ls = slice(lb * LB, (lb + 1) * LB)
                pf[j, lb, HALO : HALO + count, :] = pw[j, HALO : HALO + count, ls].astype(F32)
                edge = pw[j, 0:HALO, ls].astype(F32)
                pf[j, lb, 0:HALO, :] = jnp.where(i == 0, 0.0, edge)
            return carry

        lax.fori_loop(0, 3, body, 0)

    def short_forward():
        def body(step, carry):
            j, lb = step // lanes_n, lax.rem(step, lanes_n)
            ls = lane_slice(lb)
            taps = [jnp.broadcast_to(taps_ch[j, s : s + 1, ls], (8, LB)) for s in range(short)]
            held = [rows_apart(pf, j, lb, base - s, far_rows) for s in range(short - 1, 0, -1)]
            for q in range(far_rows):
                held.append(rows_apart(pf, j, lb, base + q, far_rows))
                total = taps[0] * held[-1]
                for s in range(1, short):
                    total = total + taps[s] * held[-1 - s]
                held = held[1:]
                mixed[j, lb, pl.ds(q, 8, stride=far_rows), :] = total.astype(BF).astype(F32)
            return carry

        lax.fori_loop(0, 3 * lanes_n, body, 0)

    def long_forward():
        def body(lb, carry):
            ls = lane_slice(lb)
            prod[:, ls] = (mixed[1, lb] * mixed[2, lb]).astype(BF)
            window = jnp.concatenate([prod[0 : 2 * long, ls], prod[long : 3 * long, ls]], axis=1)
            result = jnp.dot(fmat[group_rows(lb), :], window, preferred_element_type=F32)
            for b in range(2):
                resp[b * long : (b + 1) * long, ls] = pick(result, b)
            return carry

        lax.fori_loop(0, lanes_n, body, 0)

    kc = piece

    def project(chips, first, size):
        cols = pl.ds(first, size)
        xs = [gath[pl.ds(2 * chip, 2), :, cols].reshape(rows_chip, size) for chip in chips]
        rhs = jnp.concatenate(xs, axis=0) if len(xs) > 1 else xs[0]
        return lax.dot_general(wv[:, cols], rhs, NT, preferred_element_type=F32)

    def project_range(chips, first, last, total):
        def body(c, carry):
            return carry + project(chips, pl.multiple_of(c * kc, kc), kc)

        return lax.fori_loop(first * piece // kc, last * piece // kc, body, total)

    def keep(total, chips):
        total = total.T.astype(BF)
        for q, chip in enumerate(chips):
            rows = pl.ds(pl.multiple_of(chip * rows_chip, rows_chip), rows_chip)
            acc[rows, :] = total[q * rows_chip : (q + 1) * rows_chip]

    def branch(chips):
        for chip in chips:
            start = chip * rows_chip
            rows = pl.ds(pl.multiple_of(start, rows_chip), rows_chip)
            own = pl.ds(pl.multiple_of(start + long, rows_chip), rows_chip)
            for lb in range(lanes_n):
                ls = slice(lb * LB, (lb + 1) * LB)
                ob = acc[rows, ls].astype(F32)
                gm[0, lb, own, :] = (ob * resp[rows, ls]).astype(BF).astype(F32)
                grb[own, ls] = (ob * mixed[0, lb, own, :]).astype(BF)

    low, high = tuple(range(PIECES // 2)), tuple(range(PIECES // 2, PIECES))
    build_taps()
    build_matrix(taps_f, fmat, 0, groups)
    grb[0:long, :] = jnp.zeros((long, chan), BF)
    grb[long + count :, :] = jnp.zeros((long, chan), BF)
    for j in range(3):
        sgc[j, :, :] = jnp.zeros((8, chan), F32)
    if steps > 1:
        service(1, low)
    build_matrix(taps_b, bmat, 0, groups * 3 // 4)
    if steps > 1:
        service(1, high)
    build_matrix(taps_b, bmat, groups * 3 // 4, groups)
    if steps > 2:
        service(2, low)
        service(2, high)
    proj_copy.wait()
    halo.wait_recv()
    widen()
    short_forward()
    if steps > 2:
        service(3, low)
    long_forward()
    near = [y]
    for step in range(1, steps - 1):
        near += [chip_at(0, step), chip_at(1, step)]
    og_copy.wait()
    w_copy.wait()
    for step in range(steps - 1):
        across_arrivals(step)
    total = jnp.zeros((chan, len(near) * rows_chip), F32)
    total = project_range(near, 0, PIECES // 2, total)
    if steps > 2:
        service(3, high)
    total = project_range(near, PIECES // 2, PIECES, total)
    keep(total, near)
    branch(near)
    far = [chip_at(0, steps - 1), chip_at(0, steps), chip_at(1, steps - 1)]
    total = jnp.zeros((chan, 3 * rows_chip), F32)
    across_arrivals(steps - 1)
    for q in range(PIECES // 2):
        both = (q, q + PIECES // 2)
        service(steps, both)
        across_arrivals(steps, both)
        for chunk in both:
            total = total + project(far, chunk * piece, piece)
    keep(total, far)
    branch(far)

    back = pltpu.make_async_remote_copy(
        src_ref=grb.at[pl.ds(long, long), :],
        dst_ref=nxt,
        send_sem=halo_send.at[1],
        recv_sem=halo_recv.at[1],
        device_id={"ctx": previous},
        device_id_type=MESH,
    )

    def set_products(rows, lb, grad):
        grad = grad.astype(BF).astype(F32)
        gm[1, lb, rows, :] = (grad * mixed[2, lb, rows, :]).astype(BF).astype(F32)
        gm[2, lb, rows, :] = (grad * mixed[1, lb, rows, :]).astype(BF).astype(F32)

    def long_backward(lb):
        ls = lane_slice(lb)
        window = jnp.concatenate([grb[b * long : (b + 2) * long, ls] for b in range(3)], axis=1)
        result = jnp.dot(bmat[group_rows(lb), :], window, preferred_element_type=F32)
        for b in range(3):
            grad = pick(result, b)
            if b == 2:
                gp1[:, ls] = grad
            set_products(slice(b * long, (b + 1) * long), lb, grad)

    def short_taps(j, lb, first, apart):
        ls = lane_slice(lb)
        origin = base + first
        held = [rows_apart(pf, j, lb, origin - s, apart) for s in range(short - 1, 0, -1)]
        sums = [jnp.zeros((8, LB), F32)] * short
        for q in range(apart):
            held.append(rows_apart(pf, j, lb, origin + q, apart))
            grad = rows_apart(gm, j, lb, first + q, apart)
            sums = [sums[s] + grad * held[-1 - s] for s in range(short)]
            held = held[1:]
        for s in range(short):
            sgc[j, s : s + 1, ls] = jnp.sum(sums[s], axis=0, keepdims=True)

    def long_taps():
        flip = one_hot((long, long), lambda r, c: r + c == long - 1).astype(BF)
        wide_group = lax.broadcasted_iota(jnp.int32, (long, 2 * LB), 1) % LB // per_group

        def body(lb, carry):
            ls = lane_slice(lb)
            grads = jnp.concatenate(
                [grb[long : 2 * long, ls], grb[2 * long : 3 * long, ls]], axis=1
            )
            grads = jnp.dot(flip, grads, preferred_element_type=F32).astype(BF)
            window = jnp.concatenate([prod[0 : 2 * long, ls], prod[long : 3 * long, ls]], axis=1)
            only = [
                jnp.where(wide_group == g, grads, jnp.zeros_like(grads)) for g in range(in_block)
            ]
            table = lax.dot_general(
                jnp.concatenate(only, axis=0), window, NT, preferred_element_type=F32
            )
            sums = []
            for g in range(in_block):
                piece = table[g * long : (g + 1) * long]
                turned = pltpu.roll(piece, 0, 1, stride=1, stride_axis=0)
                sums.append(jnp.sum(turned[:, long:], axis=0, keepdims=True))
            rows = pl.ds(pl.multiple_of(lb * in_block, in_block), in_block)
            lacc[rows, :] = jnp.concatenate(sums, axis=0)
            short_taps(0, lb, long, near_rows)
            return carry

        lax.fori_loop(0, lanes_n, body, 0)

    def exchange(number, buf, me, size, peers):
        def copy(slot, d):
            return pltpu.make_async_remote_copy(
                src_ref=buf.at[slot],
                dst_ref=buf.at[slot],
                send_sem=sum_send.at[number, d - 1],
                recv_sem=sum_recv.at[number, slot],
                device_id={"ctx": peers[d - 1]},
                device_id_type=MESH,
            )

        out = [copy(me, d) for d in range(1, size)]
        order = sorted(range(size - 1), key=lambda d: -min(d + 1, size - d - 1))
        return [out[d] for d in order], [copy(lax.rem(me + d, size), d) for d in range(1, size)]

    stage_ax = exchange(0, first_x, x, nx, x_peers)
    stage_az = exchange(1, then_z, z, nz, z_peers)
    stage_bz = exchange(2, first_z, z, nz, z_peers)
    stage_bx = exchange(3, then_x, x, nx, x_peers)
    stage_sx = exchange(4, short_x, x, nx, x_peers)
    stage_sz = exchange(5, short_z, z, nz, z_peers)

    def send(stage):
        for copy in stage[0]:
            copy.start()

    def gathered(stage, buf):
        for copy in stage[1]:
            copy.wait_recv()
        total = buf[0]
        for d in range(1, buf.shape[0]):
            total = total + buf[d]
        return total

    def backward_and_taps():
        def body(lb, carry):
            long_backward(lb)
            short_taps(1, lb - 1, 0, far_rows)
            short_taps(2, lb - 1, 0, far_rows)
            return carry

        lax.fori_loop(1, lanes_n, body, 0)
        short_taps(1, lanes_n - 1, 0, far_rows)
        short_taps(2, lanes_n - 1, 0, far_rows)

    back.start()
    long_taps()
    part = groups // 2
    first_x[x, :, :] = lacc[0:part, :]
    first_z[z, :, :] = lacc[part:groups, :]
    long_backward(0)
    send(stage_ax)
    send(stage_bz)
    backward_and_taps()
    for lb in range(lanes_n):
        ls = slice(lb * LB, (lb + 1) * LB)
        head_out[:, :, ls] = gm[:, lb, long : long + 16, :].astype(BF)
    head = pltpu.make_async_remote_copy(
        src_ref=head_out,
        dst_ref=head_in,
        send_sem=halo_send.at[2],
        recv_sem=halo_recv.at[2],
        device_id={"ctx": previous},
        device_id_type=MESH,
    )
    total = jnp.zeros((8, LB), F32)
    for j in range(3):
        place = one_hot((chan, LB), lambda r, c: c - groups * j == r // per_group)
        total = total + jnp.dot(sgc[j], place, precision=HI, preferred_element_type=F32)
    short_x[x, :, :] = total
    last = i == n_ctx - 1

    def finish_backward(start, stop):
        def body(lb, carry):
            ls = lane_slice(lb)
            window = nxt[:, ls]
            window = jnp.where(last, jnp.zeros_like(window), window)
            result = jnp.dot(
                bmat[group_rows(lb), long : 2 * long], window, preferred_element_type=F32
            )
            set_products(slice(2 * long, 3 * long), lb, gp1[:, ls] + pick(result, 0))
            return carry

        lax.fori_loop(start, stop, body, 0)

    back.wait_recv()
    finish_backward(0, 1)
    send(stage_sx)
    head.start()
    then_z[z, :, :] = gathered(stage_ax, first_x)
    then_x[x, :, :] = gathered(stage_bz, first_z)
    finish_backward(1, 2)
    send(stage_az)
    send(stage_bx)
    finish_backward(2, lanes_n - 1)
    short_z[z, :, :] = gathered(stage_sx, short_x)
    finish_backward(lanes_n - 1, lanes_n)
    send(stage_sz)
    head.wait_recv()
    for lb in range(lanes_n):
        ls = slice(lb * LB, (lb + 1) * LB)
        ahead = jnp.where(last, 0.0, head_in[:, :, ls].astype(F32))
        gm[:, lb, long + count : long + count + 16, :] = ahead

    def short_backward(start, stop):
        def body(step, carry):
            j, lb = step // lanes_n, lax.rem(step, lanes_n)
            ls = lane_slice(lb)
            taps = [jnp.broadcast_to(taps_ch[j, s : s + 1, ls], (8, LB)) for s in range(short)]
            held = [rows_apart(gm, j, lb, long + s, near_rows) for s in range(short - 1)]
            for q in range(near_rows):
                held.append(rows_apart(gm, j, lb, long + q + short - 1, near_rows))
                total = taps[0] * held[0]
                for s in range(1, short):
                    total = total + taps[s] * held[s]
                held = held[1:]
                tmp[j, lb, pl.ds(q, 8, stride=near_rows), :] = total
            pgv[j, :, ls] = tmp[j, lb].astype(BF)
            return carry

        lax.fori_loop(start, stop, body, 0)

    short_backward(0, 3 * lanes_n)
    out_copy = pltpu.make_async_copy(pgv, pg_hbm, out_sem)
    out_copy.start()
    upper = gathered(stage_az, then_z)
    lower = gathered(stage_bx, then_x)
    total = jnp.concatenate([upper, lower], axis=0) * scale
    lg_ref[...] = jnp.dot(
        total,
        one_hot((long, long), lambda r, c: r + c == long - 1),
        precision=HI,
        preferred_element_type=F32,
    )
    total = gathered(stage_sz, short_z) * scale
    for j in range(3):
        place = one_hot((LB, groups), lambda r, c: r - groups * j == c)
        sums = jnp.dot(total, place, precision=HI, preferred_element_type=F32)
        sg_ref[j] = sums[0:short]

    for step in range(1, steps + 1):
        for direction in range(2):
            for chunk in chunks(direction, step):
                ring(direction, step, chunk).wait_send()
                across(direction, step, chunk, True).wait_send()
    for chunk in range(PIECES):
        across(0, 0, chunk, True).wait_send()
    halo.wait_send()
    back.wait_send()
    head.wait_send()
    for stage in (stage_ax, stage_az, stage_bz, stage_bx, stage_sx, stage_sz):
        for copy in stage[0]:
            copy.wait_send()
    out_copy.wait()


def hand_over(pg_in, sg_in, lg_in, pg_out, sg_out, lg_out, pg, sg, lg, sem_in, sem_out):
    moves = [(sg_in, sg, sg_out), (lg_in, lg, lg_out)]
    for j in range(3):
        moves.append((pg_in.at[j], pg.at[j], pg_out.at[j]))
    loads = [pltpu.make_async_copy(m[0], m[1], sem_in.at[n]) for n, m in enumerate(moves)]
    stores = [pltpu.make_async_copy(m[1], m[2], sem_out.at[n]) for n, m in enumerate(moves)]
    for copy in loads:
        copy.start()
    for load, store in zip(loads, stores):
        load.wait()
        store.start()
    for copy in stores:
        copy.wait()


def solution(mesh):
    n_ctx, n_tp = mesh.shape["ctx"], mesh.shape["tp"]
    nx = math.isqrt(n_ctx)
    nx = nx if nx * nx == n_ctx else n_ctx
    dims = (nx, n_ctx // nx, n_tp // 2)

    def step(projected, short_filter, long_filter, out_weight, out_grad):
        _, count, chan = projected.shape
        long, groups = long_filter.shape
        lanes_n = chan // LB
        most = max(dims[0], dims[1])
        part = groups // 2
        model = out_weight.shape[1]
        scale = 1.0 / math.sqrt(n_ctx * count * (chan // groups))
        steps = dims[2] // 2
        anywhere = pl.BlockSpec(memory_space=pl.ANY)
        vmem = pl.BlockSpec(memory_space=pltpu.VMEM)
        dma = pltpu.SemaphoreType.DMA
        outs = pl.pallas_call(
            functools.partial(kernel, dims, scale),
            name="hyena_backward",
            out_shape=(
                jax.ShapeDtypeStruct(projected.shape, BF),
                jax.ShapeDtypeStruct(short_filter.shape, F32),
                jax.ShapeDtypeStruct((groups, long), F32),
            ),
            in_specs=[anywhere, vmem, vmem, anywhere, anywhere],
            out_specs=(anywhere, vmem, vmem),
            scratch_shapes=[
                pltpu.VMEM((n_tp, out_grad.shape[0], model), BF),
                pltpu.VMEM((chan, model), BF),
                pltpu.VMEM((3, HALO + count, chan), BF),
                pltpu.VMEM((3, lanes_n, HALO + count, LB), F32),
                pltpu.VMEM((3, lanes_n, long + count, LB), F32),
                pltpu.VMEM((long + count, chan), BF),
                pltpu.VMEM((count, chan), F32),
                pltpu.VMEM((groups * long, 2 * long), BF),
                pltpu.VMEM((groups * long, 2 * long), BF),
                pltpu.VMEM((groups, 2 * long), F32),
                pltpu.VMEM((groups, 2 * long), F32),
                pltpu.VMEM((3, 8, chan), F32),
                pltpu.VMEM((count, chan), BF),
                pltpu.VMEM((count + 2 * long, chan), BF),
                pltpu.VMEM((long, chan), BF),
                pltpu.VMEM((3, lanes_n, long + count + 16, LB), F32),
                pltpu.VMEM((3, 16, chan), BF),
                pltpu.VMEM((3, 16, chan), BF),
                pltpu.VMEM((long, chan), F32),
                pltpu.VMEM((groups, long), F32),
                pltpu.VMEM((3, 8, chan), F32),
                pltpu.VMEM((dims[0], part, long), F32),
                pltpu.VMEM((dims[1], part, long), F32),
                pltpu.VMEM((dims[1], part, long), F32),
                pltpu.VMEM((dims[0], part, long), F32),
                pltpu.VMEM((dims[0], 8, LB), F32),
                pltpu.VMEM((dims[1], 8, LB), F32),
                pltpu.VMEM((3, lanes_n, count, LB), F32),
                pltpu.VMEM((3, count, chan), BF),
                dma((3,)),
                dma((2, steps, PIECES)),
                dma((2, steps, PIECES)),
                dma((2, steps + 1, PIECES)),
                dma((2, steps + 1, PIECES)),
                dma((3,)),
                dma((3,)),
                dma((6, max(1, most - 1))),
                dma((6, most)),
                dma,
            ],
            compiler_params=pltpu.CompilerParams(
                collective_id=0, has_side_effects=True, vmem_limit_bytes=60 * 1024 * 1024
            ),
        )(projected, short_filter, long_filter.T, out_weight, out_grad)
        outs = pl.pallas_call(
            hand_over,
            name="hand_over",
            out_shape=tuple(jax.ShapeDtypeStruct(o.shape, o.dtype) for o in outs),
            in_specs=[anywhere] * 3,
            out_specs=(anywhere,) * 3,
            scratch_shapes=[pltpu.VMEM(o.shape, o.dtype) for o in outs] + [dma((5,)), dma((5,))],
        )(*outs)
        return outs[0], outs[1], outs[2].T

    placed = (
        P(None, "ctx", "tp"),
        P(None, None, "tp"),
        P(None, "tp"),
        P("tp", None),
        P(("ctx", "tp"), None),
    )
    return jax.shard_map(
        step,
        mesh=mesh,
        in_specs=placed,
        out_specs=(P(None, "ctx", "tp"), P(None, None, "tp"), P(None, "tp")),
        check_vma=False,
    )
```

```python
import functools
import math

import jax
import jax.numpy as jnp
from jax import lax
from jax.experimental import pallas as pl
from jax.experimental.pallas import tpu as pltpu
from jax.sharding import PartitionSpec as P

MESH = pl.DeviceIdType.MESH
BF = jnp.bfloat16
F32 = jnp.float32
HALO = 144
LB = 128
PIECES = 4
NT = (((1,), (1,)), ((), ()))
HI = lax.Precision.HIGHEST


def one_hot(shape, test):
    rows = lax.broadcasted_iota(jnp.int32, shape, 0)
    cols = lax.broadcasted_iota(jnp.int32, shape, 1)
    return jnp.where(test(rows, cols), 1.0, 0.0)


def kernel(
    dims,
    scale,
    proj_hbm,
    sf_ref,
    lf_ref,
    w_hbm,
    og_hbm,
    pg_hbm,
    sg_ref,
    lg_ref,
    gath,
    wv,
    pw,
    pf,
    mixed,
    prod,
    resp,
    fmat,
    bmat,
    taps_f,
    taps_b,
    taps_ch,
    acc,
    grb,
    nxt,
    gm,
    head_out,
    head_in,
    gp1,
    lacc,
    sgc,
    first_x,
    then_z,
    first_z,
    then_x,
    short_x,
    short_z,
    tmp,
    pgv,
    local_sem,
    ring_send,
    ring_recv,
    sib_send,
    sib_recv,
    halo_send,
    halo_recv,
    sum_send,
    sum_recv,
    out_sem,
):
    nx, nz, ny = dims
    n_ctx = nx * nz
    i = lax.axis_index("ctx")
    k = lax.axis_index("tp")
    x, z = lax.rem(i, nx), i // nx
    y, core = k // 2, lax.rem(k, 2)
    count = proj_hbm.shape[1]
    chan = proj_hbm.shape[2]
    model = w_hbm.shape[1]
    short = sf_ref.shape[1]
    groups, long = lf_ref.shape
    per_group = chan // groups
    lanes_n = chan // LB
    in_block = LB // per_group
    rows_chip = 2 * og_hbm.shape[0]
    piece = model // PIECES

    right = lax.rem(y + 1, ny) * 2 + core
    left = lax.rem(y + ny - 1, ny) * 2 + core
    sibling = y * 2 + 1 - core
    following = lax.rem(i + 1, n_ctx)
    previous = lax.rem(i + n_ctx - 1, n_ctx)
    x_peers = [z * nx + lax.rem(x + d, nx) for d in range(1, nx)]
    z_peers = [lax.rem(z + d, nz) * nx + x for d in range(1, nz)]

    barrier = pltpu.get_barrier_semaphore()
    tp_greet = [right, left, sibling]
    ctx_greet = [following, previous] + x_peers + z_peers
    for other in tp_greet:
        pl.semaphore_signal(barrier, inc=1, device_id={"tp": other}, device_id_type=MESH)
    for other in ctx_greet:
        pl.semaphore_signal(barrier, inc=1, device_id={"ctx": other}, device_id_type=MESH)

    og_copy = pltpu.make_async_copy(og_hbm, gath.at[k], local_sem.at[0])
    og_copy.start()
    proj_copy = pltpu.make_async_copy(proj_hbm, pw.at[:, pl.ds(HALO, count), :], local_sem.at[1])
    proj_copy.start()
    w_copy = pltpu.make_async_copy(w_hbm, wv, local_sem.at[2])
    w_copy.start()
    pl.semaphore_wait(barrier, len(tp_greet) + len(ctx_greet))

    steps = ny // 2

    def chunks(direction, step):
        if step < steps:
            return tuple(range(PIECES))
        return tuple(range(direction * PIECES // 2, (direction + 1) * PIECES // 2))

    def chip_at(direction, distance):
        if direction == 0:
            return lax.rem(y + ny - distance, ny)
        return lax.rem(y + distance, ny)

    def columns(chunk):
        return pl.ds(chunk * piece, piece)

    def ring(direction, step, chunk, arriving=False):
        block = chip_at(direction, step if arriving else step - 1) * 2 + core
        ref = gath.at[block, :, columns(chunk)]
        own = step == 1 and not arriving
        return pltpu.make_async_remote_copy(
            src_ref=og_hbm.at[:, columns(chunk)] if own else ref,
            dst_ref=ref,
            send_sem=ring_send.at[direction, step - 1, chunk],
            recv_sem=ring_recv.at[direction, step - 1, chunk],
            device_id={"tp": right if direction == 0 else left},
            device_id_type=MESH,
        )

    def across(direction, step, chunk, own):
        block = chip_at(direction, step) * 2 + (core if own else 1 - core)
        ref = gath.at[block, :, columns(chunk)]
        return pltpu.make_async_remote_copy(
            src_ref=og_hbm.at[:, columns(chunk)] if own and step == 0 else ref,
            dst_ref=ref,
            send_sem=sib_send.at[direction, step, chunk],
            recv_sem=sib_recv.at[direction, step, chunk],
            device_id={"tp": sibling},
            device_id_type=MESH,
        )

    for chunk in range(PIECES):
        for direction in range(2):
            if chunk in chunks(direction, 1):
                ring(direction, 1, chunk).start()
    halo = pltpu.make_async_remote_copy(
        src_ref=proj_hbm.at[:, pl.ds(count - HALO, HALO), :],
        dst_ref=pw.at[:, pl.ds(0, HALO), :],
        send_sem=halo_send.at[0],
        recv_sem=halo_recv.at[0],
        device_id={"ctx": following},
        device_id_type=MESH,
    )
    halo.start()
    for chunk in range(PIECES):
        across(0, 0, chunk, True).start()

    def service(step, which):
        for chunk in which:
            for direction in range(2):
                if chunk in chunks(direction, step):
                    ring(direction, step, chunk, True).wait_recv()
                    if step < steps and chunk in chunks(direction, step + 1):
                        ring(direction, step + 1, chunk).start()
                    across(direction, step, chunk, True).start()

    def across_arrivals(step, which=tuple(range(PIECES))):
        for direction in range(2 if step > 0 else 1):
            for chunk in chunks(direction, step):
                if chunk in which:
                    across(direction, step, chunk, False).wait_recv()

    def build_taps():
        spread = one_hot((groups, chan), lambda r, c: c // per_group == r)
        for j in range(3):
            taps_ch[j, 0:short, :] = jnp.dot(
                sf_ref[j], spread, precision=HI, preferred_element_type=F32
            )
        lf = lf_ref[...]
        backwards = one_hot((long, 2 * long), lambda r, c: c == long - r).astype(BF)
        taps_f[...] = jnp.dot(lf, backwards, preferred_element_type=F32)
        taps_b[:, 0:long] = lf.astype(F32)
        taps_b[:, long:] = jnp.zeros((groups, long), F32)

    def build_matrix(taps, matrix, start, stop):
        def body(g, carry):
            row = jnp.broadcast_to(taps[pl.ds(g, 1), :], (long, 2 * long))
            turned = pltpu.roll(row, 0, 1, stride=1, stride_axis=0)
            matrix[pl.ds(pl.multiple_of(g * long, long), long), :] = turned.astype(BF)
            return carry

        lax.fori_loop(start, stop, body, 0)

    lane_group = lax.broadcasted_iota(jnp.int32, (long, LB), 1) // per_group

    def pick(result, b):
        total = jnp.zeros((long, LB), F32)
        for g in range(in_block):
            piece = result[g * long : (g + 1) * long, b * LB : (b + 1) * LB]
            total = jnp.where(lane_group == g, piece, total)
        return total

    def lane_slice(lb):
        return pl.ds(lb * LB if isinstance(lb, int) else pl.multiple_of(lb * LB, LB), LB)

    def group_rows(lb):
        size = in_block * long
        return pl.ds(lb * size if isinstance(lb, int) else pl.multiple_of(lb * size, size), size)

    base = HALO - long
    far_rows = (long + count) // 8
    near_rows = count // 8

    def rows_apart(ref, j, lb, first, stride):
        return ref[j, lb, pl.ds(first, 8, stride=stride), :]

    def widen():
        def body(j, carry):
            for lb in range(lanes_n):
                ls = slice(lb * LB, (lb + 1) * LB)
                pf[j, lb, HALO : HALO + count, :] = pw[j, HALO : HALO + count, ls].astype(F32)
                edge = pw[j, 0:HALO, ls].astype(F32)
                pf[j, lb, 0:HALO, :] = jnp.where(i == 0, 0.0, edge)
            return carry

        lax.fori_loop(0, 3, body, 0)

    def short_forward():
        def body(step, carry):
            j, lb = step // lanes_n, lax.rem(step, lanes_n)
            ls = lane_slice(lb)
            taps = [jnp.broadcast_to(taps_ch[j, s : s + 1, ls], (8, LB)) for s in range(short)]
            held = [rows_apart(pf, j, lb, base - s, far_rows) for s in range(short - 1, 0, -1)]
            for q in range(far_rows):
                held.append(rows_apart(pf, j, lb, base + q, far_rows))
                total = taps[0] * held[-1]
                for s in range(1, short):
                    total = total + taps[s] * held[-1 - s]
                held = held[1:]
                mixed[j, lb, pl.ds(q, 8, stride=far_rows), :] = total.astype(BF).astype(F32)
            return carry

        lax.fori_loop(0, 3 * lanes_n, body, 0)

    def long_forward():
        def body(lb, carry):
            ls = lane_slice(lb)
            prod[:, ls] = (mixed[1, lb] * mixed[2, lb]).astype(BF)
            window = jnp.concatenate([prod[0 : 2 * long, ls], prod[long : 3 * long, ls]], axis=1)
            result = jnp.dot(fmat[group_rows(lb), :], window, preferred_element_type=F32)
            for b in range(2):
                resp[b * long : (b + 1) * long, ls] = pick(result, b)
            return carry

        lax.fori_loop(0, lanes_n, body, 0)

    kc = piece

    def project(chips, first, size):
        cols = pl.ds(first, size)
        xs = [gath[pl.ds(2 * chip, 2), :, cols].reshape(rows_chip, size) for chip in chips]
        rhs = jnp.concatenate(xs, axis=0) if len(xs) > 1 else xs[0]
        return lax.dot_general(wv[:, cols], rhs, NT, preferred_element_type=F32)

    def project_range(chips, first, last, total):
        def body(c, carry):
            return carry + project(chips, pl.multiple_of(c * kc, kc), kc)

        return lax.fori_loop(first * piece // kc, last * piece // kc, body, total)

    def keep(total, chips):
        total = total.T.astype(BF)
        for q, chip in enumerate(chips):
            rows = pl.ds(pl.multiple_of(chip * rows_chip, rows_chip), rows_chip)
            acc[rows, :] = total[q * rows_chip : (q + 1) * rows_chip]

    def branch(chips):
        for chip in chips:
            start = chip * rows_chip
            rows = pl.ds(pl.multiple_of(start, rows_chip), rows_chip)
            own = pl.ds(pl.multiple_of(start + long, rows_chip), rows_chip)
            for lb in range(lanes_n):
                ls = slice(lb * LB, (lb + 1) * LB)
                ob = acc[rows, ls].astype(F32)
                gm[0, lb, own, :] = (ob * resp[rows, ls]).astype(BF).astype(F32)
                grb[own, ls] = (ob * mixed[0, lb, own, :]).astype(BF)

    low, high = tuple(range(PIECES // 2)), tuple(range(PIECES // 2, PIECES))
    build_taps()
    build_matrix(taps_f, fmat, 0, groups)
    grb[0:long, :] = jnp.zeros((long, chan), BF)
    grb[long + count :, :] = jnp.zeros((long, chan), BF)
    for j in range(3):
        sgc[j, :, :] = jnp.zeros((8, chan), F32)
    if steps > 1:
        service(1, low)
    build_matrix(taps_b, bmat, 0, groups * 3 // 4)
    if steps > 1:
        service(1, high)
    build_matrix(taps_b, bmat, groups * 3 // 4, groups)
    if steps > 2:
        service(2, low)
        service(2, high)
    proj_copy.wait()
    halo.wait_recv()
    widen()
    short_forward()
    if steps > 2:
        service(3, low)
    long_forward()
    near = [y]
    for step in range(1, steps - 1):
        near += [chip_at(0, step), chip_at(1, step)]
    og_copy.wait()
    w_copy.wait()
    for step in range(steps - 1):
        across_arrivals(step)
    total = jnp.zeros((chan, len(near) * rows_chip), F32)
    total = project_range(near, 0, PIECES // 2, total)
    if steps > 2:
        service(3, high)
    total = project_range(near, PIECES // 2, PIECES, total)
    keep(total, near)
    branch(near)
    far = [chip_at(0, steps - 1), chip_at(0, steps), chip_at(1, steps - 1)]
    total = jnp.zeros((chan, 3 * rows_chip), F32)
    across_arrivals(steps - 1)
    for q in range(PIECES // 2):
        both = (q, q + PIECES // 2)
        service(steps, both)
        across_arrivals(steps, both)
        for chunk in both:
            total = total + project(far, chunk * piece, piece)
    keep(total, far)
    branch(far)

    back = pltpu.make_async_remote_copy(
        src_ref=grb.at[pl.ds(long, long), :],
        dst_ref=nxt,
        send_sem=halo_send.at[1],
        recv_sem=halo_recv.at[1],
        device_id={"ctx": previous},
        device_id_type=MESH,
    )

    def set_products(rows, lb, grad):
        grad = grad.astype(BF).astype(F32)
        gm[1, lb, rows, :] = (grad * mixed[2, lb, rows, :]).astype(BF).astype(F32)
        gm[2, lb, rows, :] = (grad * mixed[1, lb, rows, :]).astype(BF).astype(F32)

    def long_backward(lb):
        ls = lane_slice(lb)
        window = jnp.concatenate([grb[b * long : (b + 2) * long, ls] for b in range(3)], axis=1)
        result = jnp.dot(bmat[group_rows(lb), :], window, preferred_element_type=F32)
        for b in range(3):
            grad = pick(result, b)
            if b == 2:
                gp1[:, ls] = grad
            set_products(slice(b * long, (b + 1) * long), lb, grad)

    def short_taps(j, lb, first, apart):
        ls = lane_slice(lb)
        origin = base + first
        held = [rows_apart(pf, j, lb, origin - s, apart) for s in range(short - 1, 0, -1)]
        sums = [jnp.zeros((8, LB), F32)] * short
        for q in range(apart):
            held.append(rows_apart(pf, j, lb, origin + q, apart))
            grad = rows_apart(gm, j, lb, first + q, apart)
            sums = [sums[s] + grad * held[-1 - s] for s in range(short)]
            held = held[1:]
        for s in range(short):
            sgc[j, s : s + 1, ls] = jnp.sum(sums[s], axis=0, keepdims=True)

    def long_taps():
        flip = one_hot((long, long), lambda r, c: r + c == long - 1).astype(BF)
        wide_group = lax.broadcasted_iota(jnp.int32, (long, 2 * LB), 1) % LB // per_group

        def body(lb, carry):
            ls = lane_slice(lb)
            grads = jnp.concatenate(
                [grb[long : 2 * long, ls], grb[2 * long : 3 * long, ls]], axis=1
            )
            grads = jnp.dot(flip, grads, preferred_element_type=F32).astype(BF)
            window = jnp.concatenate([prod[0 : 2 * long, ls], prod[long : 3 * long, ls]], axis=1)
            only = [
                jnp.where(wide_group == g, grads, jnp.zeros_like(grads)) for g in range(in_block)
            ]
            table = lax.dot_general(
                jnp.concatenate(only, axis=0), window, NT, preferred_element_type=F32
            )
            sums = []
            for g in range(in_block):
                piece = table[g * long : (g + 1) * long]
                turned = pltpu.roll(piece, 0, 1, stride=1, stride_axis=0)
                sums.append(jnp.sum(turned[:, long:], axis=0, keepdims=True))
            rows = pl.ds(pl.multiple_of(lb * in_block, in_block), in_block)
            lacc[rows, :] = jnp.concatenate(sums, axis=0)
            short_taps(0, lb, long, near_rows)
            return carry

        lax.fori_loop(0, lanes_n, body, 0)

    def exchange(number, buf, me, size, peers):
        def copy(slot, d):
            return pltpu.make_async_remote_copy(
                src_ref=buf.at[slot],
                dst_ref=buf.at[slot],
                send_sem=sum_send.at[number, d - 1],
                recv_sem=sum_recv.at[number, slot],
                device_id={"ctx": peers[d - 1]},
                device_id_type=MESH,
            )

        out = [copy(me, d) for d in range(1, size)]
        order = sorted(range(size - 1), key=lambda d: -min(d + 1, size - d - 1))
        return [out[d] for d in order], [copy(lax.rem(me + d, size), d) for d in range(1, size)]

    stage_ax = exchange(0, first_x, x, nx, x_peers)
    stage_az = exchange(1, then_z, z, nz, z_peers)
    stage_bz = exchange(2, first_z, z, nz, z_peers)
    stage_bx = exchange(3, then_x, x, nx, x_peers)
    stage_sx = exchange(4, short_x, x, nx, x_peers)
    stage_sz = exchange(5, short_z, z, nz, z_peers)

    def send(stage):
        for copy in stage[0]:
            copy.start()

    def gathered(stage, buf):
        for copy in stage[1]:
            copy.wait_recv()
        total = buf[0].astype(F32)
        for d in range(1, buf.shape[0]):
            total = total + buf[d].astype(F32)
        return total

    def backward_and_taps():
        def body(lb, carry):
            long_backward(lb)
            short_taps(1, lb - 1, 0, far_rows)
            short_taps(2, lb - 1, 0, far_rows)
            return carry

        lax.fori_loop(1, lanes_n, body, 0)
        short_taps(1, lanes_n - 1, 0, far_rows)
        short_taps(2, lanes_n - 1, 0, far_rows)

    back.start()
    long_taps()
    part = groups // 2
    first_x[x, :, :] = lacc[0:part, :].astype(BF)
    first_z[z, :, :] = lacc[part:groups, :].astype(BF)
    long_backward(0)
    send(stage_ax)
    send(stage_bz)
    backward_and_taps()
    for lb in range(lanes_n):
        ls = slice(lb * LB, (lb + 1) * LB)
        head_out[:, :, ls] = gm[:, lb, long : long + 16, :].astype(BF)
    head = pltpu.make_async_remote_copy(
        src_ref=head_out,
        dst_ref=head_in,
        send_sem=halo_send.at[2],
        recv_sem=halo_recv.at[2],
        device_id={"ctx": previous},
        device_id_type=MESH,
    )
    total = jnp.zeros((8, LB), F32)
    for j in range(3):
        place = one_hot((chan, LB), lambda r, c: c - groups * j == r // per_group)
        total = total + jnp.dot(sgc[j], place, precision=HI, preferred_element_type=F32)
    short_x[x, :, :] = total
    last = i == n_ctx - 1

    def finish_backward(start, stop):
        def body(lb, carry):
            ls = lane_slice(lb)
            window = nxt[:, ls]
            window = jnp.where(last, jnp.zeros_like(window), window)
            result = jnp.dot(
                bmat[group_rows(lb), long : 2 * long], window, preferred_element_type=F32
            )
            set_products(slice(2 * long, 3 * long), lb, gp1[:, ls] + pick(result, 0))
            return carry

        lax.fori_loop(start, stop, body, 0)

    back.wait_recv()
    finish_backward(0, 1)
    send(stage_sx)
    head.start()
    then_z[z, :, :] = gathered(stage_ax, first_x).astype(BF)
    then_x[x, :, :] = gathered(stage_bz, first_z).astype(BF)
    finish_backward(1, 2)
    send(stage_az)
    send(stage_bx)
    finish_backward(2, lanes_n - 1)
    short_z[z, :, :] = gathered(stage_sx, short_x)
    finish_backward(lanes_n - 1, lanes_n)
    send(stage_sz)
    head.wait_recv()
    for lb in range(lanes_n):
        ls = slice(lb * LB, (lb + 1) * LB)
        ahead = jnp.where(last, 0.0, head_in[:, :, ls].astype(F32))
        gm[:, lb, long + count : long + count + 16, :] = ahead

    def short_backward(start, stop):
        def body(step, carry):
            j, lb = step // lanes_n, lax.rem(step, lanes_n)
            ls = lane_slice(lb)
            taps = [jnp.broadcast_to(taps_ch[j, s : s + 1, ls], (8, LB)) for s in range(short)]
            held = [rows_apart(gm, j, lb, long + s, near_rows) for s in range(short - 1)]
            for q in range(near_rows):
                held.append(rows_apart(gm, j, lb, long + q + short - 1, near_rows))
                total = taps[0] * held[0]
                for s in range(1, short):
                    total = total + taps[s] * held[s]
                held = held[1:]
                tmp[j, lb, pl.ds(q, 8, stride=near_rows), :] = total
            pgv[j, :, ls] = tmp[j, lb].astype(BF)
            return carry

        lax.fori_loop(start, stop, body, 0)

    short_backward(0, 3 * lanes_n)
    out_copy = pltpu.make_async_copy(pgv, pg_hbm, out_sem)
    out_copy.start()
    upper = gathered(stage_az, then_z)
    lower = gathered(stage_bx, then_x)
    total = jnp.concatenate([upper, lower], axis=0) * scale
    lg_ref[...] = jnp.dot(
        total,
        one_hot((long, long), lambda r, c: r + c == long - 1),
        precision=HI,
        preferred_element_type=F32,
    )
    total = gathered(stage_sz, short_z) * scale
    for j in range(3):
        place = one_hot((LB, groups), lambda r, c: r - groups * j == c)
        sums = jnp.dot(total, place, precision=HI, preferred_element_type=F32)
        sg_ref[j] = sums[0:short]

    for step in range(1, steps + 1):
        for direction in range(2):
            for chunk in chunks(direction, step):
                ring(direction, step, chunk).wait_send()
                across(direction, step, chunk, True).wait_send()
    for chunk in range(PIECES):
        across(0, 0, chunk, True).wait_send()
    halo.wait_send()
    back.wait_send()
    head.wait_send()
    for stage in (stage_ax, stage_az, stage_bz, stage_bx, stage_sx, stage_sz):
        for copy in stage[0]:
            copy.wait_send()
    out_copy.wait()


def hand_over(pg_in, sg_in, lg_in, pg_out, sg_out, lg_out, pg, sg, lg, sem_in, sem_out):
    moves = [(sg_in, sg, sg_out), (lg_in, lg, lg_out)]
    for j in range(3):
        moves.append((pg_in.at[j], pg.at[j], pg_out.at[j]))
    loads = [pltpu.make_async_copy(m[0], m[1], sem_in.at[n]) for n, m in enumerate(moves)]
    stores = [pltpu.make_async_copy(m[1], m[2], sem_out.at[n]) for n, m in enumerate(moves)]
    for copy in loads:
        copy.start()
    for load, store in zip(loads, stores):
        load.wait()
        store.start()
    for copy in stores:
        copy.wait()


def solution(mesh):
    n_ctx, n_tp = mesh.shape["ctx"], mesh.shape["tp"]
    nx = math.isqrt(n_ctx)
    nx = nx if nx * nx == n_ctx else n_ctx
    dims = (nx, n_ctx // nx, n_tp // 2)

    def step(projected, short_filter, long_filter, out_weight, out_grad):
        _, count, chan = projected.shape
        long, groups = long_filter.shape
        lanes_n = chan // LB
        most = max(dims[0], dims[1])
        part = groups // 2
        model = out_weight.shape[1]
        scale = 1.0 / math.sqrt(n_ctx * count * (chan // groups))
        steps = dims[2] // 2
        anywhere = pl.BlockSpec(memory_space=pl.ANY)
        vmem = pl.BlockSpec(memory_space=pltpu.VMEM)
        dma = pltpu.SemaphoreType.DMA
        outs = pl.pallas_call(
            functools.partial(kernel, dims, scale),
            name="hyena_backward",
            out_shape=(
                jax.ShapeDtypeStruct(projected.shape, BF),
                jax.ShapeDtypeStruct(short_filter.shape, F32),
                jax.ShapeDtypeStruct((groups, long), F32),
            ),
            in_specs=[anywhere, vmem, vmem, anywhere, anywhere],
            out_specs=(anywhere, vmem, vmem),
            scratch_shapes=[
                pltpu.VMEM((n_tp, out_grad.shape[0], model), BF),
                pltpu.VMEM((chan, model), BF),
                pltpu.VMEM((3, HALO + count, chan), BF),
                pltpu.VMEM((3, lanes_n, HALO + count, LB), F32),
                pltpu.VMEM((3, lanes_n, long + count, LB), F32),
                pltpu.VMEM((long + count, chan), BF),
                pltpu.VMEM((count, chan), F32),
                pltpu.VMEM((groups * long, 2 * long), BF),
                pltpu.VMEM((groups * long, 2 * long), BF),
                pltpu.VMEM((groups, 2 * long), F32),
                pltpu.VMEM((groups, 2 * long), F32),
                pltpu.VMEM((3, 8, chan), F32),
                pltpu.VMEM((count, chan), BF),
                pltpu.VMEM((count + 2 * long, chan), BF),
                pltpu.VMEM((long, chan), BF),
                pltpu.VMEM((3, lanes_n, long + count + 16, LB), F32),
                pltpu.VMEM((3, 16, chan), BF),
                pltpu.VMEM((3, 16, chan), BF),
                pltpu.VMEM((long, chan), F32),
                pltpu.VMEM((groups, long), F32),
                pltpu.VMEM((3, 8, chan), F32),
                pltpu.VMEM((dims[0], part, long), BF),
                pltpu.VMEM((dims[1], part, long), BF),
                pltpu.VMEM((dims[1], part, long), BF),
                pltpu.VMEM((dims[0], part, long), BF),
                pltpu.VMEM((dims[0], 8, LB), F32),
                pltpu.VMEM((dims[1], 8, LB), F32),
                pltpu.VMEM((3, lanes_n, count, LB), F32),
                pltpu.VMEM((3, count, chan), BF),
                dma((3,)),
                dma((2, steps, PIECES)),
                dma((2, steps, PIECES)),
                dma((2, steps + 1, PIECES)),
                dma((2, steps + 1, PIECES)),
                dma((3,)),
                dma((3,)),
                dma((6, max(1, most - 1))),
                dma((6, most)),
                dma,
            ],
            compiler_params=pltpu.CompilerParams(
                collective_id=0, has_side_effects=True, vmem_limit_bytes=60 * 1024 * 1024
            ),
        )(projected, short_filter, long_filter.T, out_weight, out_grad)
        outs = pl.pallas_call(
            hand_over,
            name="hand_over",
            out_shape=tuple(jax.ShapeDtypeStruct(o.shape, o.dtype) for o in outs),
            in_specs=[anywhere] * 3,
            out_specs=(anywhere,) * 3,
            scratch_shapes=[pltpu.VMEM(o.shape, o.dtype) for o in outs] + [dma((5,)), dma((5,))],
        )(*outs)
        return outs[0], outs[1], outs[2].T

    placed = (
        P(None, "ctx", "tp"),
        P(None, None, "tp"),
        P(None, "tp"),
        P("tp", None),
        P(("ctx", "tp"), None),
    )
    return jax.shard_map(
        step,
        mesh=mesh,
        in_specs=placed,
        out_specs=(P(None, "ctx", "tp"), P(None, None, "tp"), P(None, "tp")),
        check_vma=False,
    )
```
